32 devices in a mesh: scan: 8 (over z, x), bin: 4 (over y, core).
Axes of the slice: x: 2, y: 2, z: 4, core: 2. Of those that a mesh axis runs over, the one named last changes fastest.
Arguments:
- tile_blocks: bfloat16 [64, 16, 256, 256], P('scan', 'bin'), may hold values from -0.25 to 0.25
- tile_pattern: int32 [2, 64], P(None, 'scan'), may hold values from 0 to 63, as said below
- tile_count: int32 [8], P('scan'), may hold values from 1 to 8, as said below
- initial_map: float32 [16, 4, 4096], P('bin', None, 'scan')
- measured: float32 [16, 4, 16384], P('bin', None, 'scan')
- step_size: float32 [1], replicated, may hold values from 0.06 to 0.1
- penalty: float32 [4096], P('scan'), may hold values from 40 to 200
Outputs:
- source_map: float32 [16, 4, 4096], P('bin', None, 'scan')
The draws below stay inside these ranges and needn't reach their ends.
Inputs may be any that keep to these rules, and one draw needn't show every extreme that they name: `tile_pattern`: row 0 names a sensor block of 64; row 1 of slot s names one of the 2 scan tiles (s // 8) * 2 to (s // 8) * 2 + 1. Only the first tile_count[d] slots of index d of scan are live; in every draw some indices have all 8 slots live.
All inputs are finite; a program needn't handle non-finite values.
Results may differ from the reference program's by a relative error of at most 0.00074.
Values may be sent and summed in bfloat16 or wider, within the bound.
No kernel may reach another device: no remote copies, remote signals or barrier semaphores. Data moves between devices by JAX's collectives and lax.ppermute only.
A program may use at most 64 MiB of HBM per device.

```python
import math
import jax
import jax.numpy as jnp
from jax import lax

BINS = 16
SNAP = 4
SENSORS = 16384
TILE = 256
TILE_DEV = 2
ITERS = 2
CAP = 8
GROUPS = 8
SLOTS = 64
POINTS = 4096


def bin_scales(lowest, ratio):
    levels = jnp.arange(BINS, dtype=jnp.float32) / (BINS - 1)
    return lowest * ratio ** levels


def draw_tile_pattern(key, part):
    key_cols, key_rows, key_pick = jax.random.split(jax.random.fold_in(key, 3), 3)
    slot_ids = jnp.arange(SLOTS, dtype=jnp.int32)
    owners = slot_ids // CAP
    offsets = jax.random.randint(key_cols, (GROUPS,), 0, TILE_DEV, dtype=jnp.int32)[owners]
    columns = owners * TILE_DEV + (slot_ids + offsets) % TILE_DEV
    blocks_all = SENSORS // TILE
    sensor_rows = jax.random.randint(key_rows, (SLOTS,), 0, blocks_all, dtype=jnp.int32)
    chosen = jax.random.randint(key_pick, (), 0, SLOTS, dtype=jnp.int32)
    sensor_rows = jnp.where(slot_ids == chosen, blocks_all - 1, sensor_rows)
    return jnp.stack([sensor_rows, columns]).astype(jnp.int32)


def draw_tile_count(key, part):
    key_light, key_heavy, key_pick = jax.random.split(jax.random.fold_in(key, 5), 3)
    light = jax.random.randint(key_light, (GROUPS,), 1, 4, dtype=jnp.int32)
    heavy = jax.random.randint(key_heavy, (GROUPS,), 0, 4, dtype=jnp.int32) == 0
    chosen = jax.random.randint(key_pick, (), 0, GROUPS, dtype=jnp.int32)
    heavy = jnp.logical_or(heavy, jnp.arange(GROUPS, dtype=jnp.int32) == chosen)
    return jnp.where(heavy, CAP, light).astype(jnp.int32)


def draw_initial_map(key, part):
    key_base, key_snap = jax.random.split(jax.random.fold_in(key, 7))
    base = jax.random.truncated_normal(key_base, -3.0, 3.0, (BINS, SNAP, POINTS), jnp.float32)
    snapshot = jax.random.uniform(key_snap, (1, SNAP, 1), jnp.float32, 0.5, 2.0)
    return (base * snapshot * bin_scales(0.316, 10.0)[:, None, None]).astype(jnp.float32)


def draw_measured(key, part):
    key_base = jax.random.fold_in(jax.random.fold_in(key, 9), 0)
    base = jax.random.truncated_normal(key_base, -3.0, 3.0, (BINS, SNAP, SENSORS), jnp.float32)
    return (base * bin_scales(0.6, 3.0)[:, None, None]).astype(jnp.float32)


def steps_of(rng, extent, cuts, smallest, top_value):
    def one(position, parts):
        draws = jax.random.uniform(jax.random.fold_in(jax.random.fold_in(rng, 6), position), (parts,), jnp.float32, smallest / len(cuts), top_value / len(cuts))
        return jnp.repeat(jnp.exp(draws), extent[position] // parts).reshape((-1,) + (1,) * (len(extent) - position - 1))

    level = one(*cuts[0])
    for cut in cuts[1:]:
        level = level * one(*cut)
    return level


def noise(own_key, extent, spread, most, cuts=(), held_as=jnp.bfloat16):
    loudness = steps_of(own_key, extent, cuts, -0.22, 0.18) if cuts else 1.0
    entries = jax.random.normal(own_key, extent, jnp.float32) * spread * loudness
    return jnp.minimum(jnp.maximum(entries, -most), most).astype(held_as)


def setup_inputs(seed: int = 0) -> dict:
    arg_keys = jax.random.split(jax.random.key(seed), 8)
    return {
        "tile_blocks": noise(arg_keys[0], (SLOTS, BINS, TILE, TILE), (2 * TILE) ** -0.5, 0.25, ((0, 8), (1, 4))),
        "tile_pattern": draw_tile_pattern(jax.random.fold_in(arg_keys[7], 71), 0),
        "tile_count": draw_tile_count(jax.random.fold_in(arg_keys[7], 71), 0),
        "initial_map": draw_initial_map(jax.random.fold_in(arg_keys[7], 71), 0),
        "measured": draw_measured(jax.random.fold_in(arg_keys[7], 71), 0),
        "step_size": jnp.clip(jax.random.uniform(arg_keys[5], (1,), jnp.float32, 0.06, 0.1), 0.06, 0.1),
        "penalty": jnp.clip(jnp.exp(math.log(200.0) - 1.609438 * jax.random.uniform(arg_keys[6], (POINTS,), jnp.float32) ** steps_of(arg_keys[6], (POINTS,), ((0, 8),), -0.2, 0.2)), 40.0, 200.0),
    }


def reference(tile_blocks, tile_pattern, tile_count, initial_map, measured, step_size, penalty):
    slot_ids = jnp.arange(SLOTS, dtype=jnp.int32)
    live_mask = (slot_ids % CAP < tile_count[slot_ids // CAP]).astype(jnp.float32)
    block_rows = tile_pattern[0].astype(jnp.int32)
    block_cols = tile_pattern[1].astype(jnp.int32)
    current = initial_map
    for iteration in range(ITERS):
        rounded_map = current.astype(jnp.bfloat16).astype(jnp.float32)

        def forward(running, slot_id):
            matrix = tile_blocks[slot_id].astype(jnp.float32)
            source = lax.dynamic_slice_in_dim(rounded_map, block_cols[slot_id] * TILE, TILE, 2)
            contrib = jnp.einsum('fij,fsj->fsi', matrix, source) * live_mask[slot_id]
            start = block_rows[slot_id] * TILE
            present = lax.dynamic_slice_in_dim(running, start, TILE, 2)
            return (lax.dynamic_update_slice_in_dim(running, present + contrib, start, 2), None)
        predicted = lax.scan(forward, jnp.zeros((BINS, SNAP, SENSORS), jnp.float32), slot_ids)[0]
        residual = predicted - measured
        rounded_residual = residual.astype(jnp.bfloat16).astype(jnp.float32)

        def backward(running, slot_id):
            matrix = tile_blocks[slot_id].astype(jnp.float32)
            source = lax.dynamic_slice_in_dim(rounded_residual, block_rows[slot_id] * TILE, TILE, 2)
            contrib = jnp.einsum('fij,fsi->fsj', matrix, source) * live_mask[slot_id]
            start = block_cols[slot_id] * TILE
            present = lax.dynamic_slice_in_dim(running, start, TILE, 2)
            return (lax.dynamic_update_slice_in_dim(running, present + contrib, start, 2), None)
        gradient = lax.scan(backward, jnp.zeros((BINS, SNAP, POINTS), jnp.float32), slot_ids)[0]
        moved = current - step_size[0] * gradient
        energy = lax.optimization_barrier(jnp.sum(moved * moved, axis=(0, 1)))
        current = moved * jnp.maximum(0.0, 1.0 - step_size[0] * penalty / jnp.sqrt(energy + 1e-06))
    return current
```

```python
import functools

import jax
import jax.numpy as jnp
from jax import lax
from jax.experimental import pallas as pl
from jax.experimental.pallas import tpu as pltpu
from jax.sharding import PartitionSpec as P

ITERS = 2
F32 = jnp.float32
BF16 = jnp.bfloat16


def vmem():
    return pl.BlockSpec(memory_space=pltpu.VMEM)


def smem():
    return pl.BlockSpec(memory_space=pltpu.SMEM)


def masked_rows(value, bins, snaps):
    row = lax.broadcasted_iota(jnp.int32, value.shape, 0) // snaps
    return [jnp.where(row == f, value, 0.0).astype(BF16) for f in range(bins)]


def column(pattern_ref, s, points, tile):
    return pl.multiple_of(lax.rem(pattern_ref[1, s], points // tile) * tile, tile)


def forward_slot(s, pattern_ref, xm_ref, a_ref, c_ref, cb_ref):
    slots, bins, tile = a_ref.shape[0], a_ref.shape[1], a_ref.shape[-1]
    start = column(pattern_ref, s, xm_ref.shape[-1], tile)
    total = None
    for f in range(bins):
        part = lax.dot_general(
            xm_ref[f, :, pl.ds(start, tile)],
            a_ref[s, f],
            (((1,), (1,)), ((), ())),
            preferred_element_type=F32,
        )
        total = part if total is None else total + part
    c_ref[s] = total
    cb_ref[s] = total.astype(BF16)


def first_kernel(pattern_ref, x_ref, a_ref, cur_ref, c_ref, cb_ref, xm_ref):
    slots, bins = a_ref.shape[0], a_ref.shape[1]
    snaps = x_ref.shape[1]
    value = jnp.concatenate([x_ref[f] for f in range(bins)], axis=0)
    cur_ref[...] = value
    for f, part in enumerate(masked_rows(value, bins, snaps)):
        xm_ref[f] = part
    for s in range(slots):
        forward_slot(s, pattern_ref, xm_ref, a_ref, c_ref, cb_ref)


def send_kernel(pattern_ref, count_ref, m_ref, out_ref):
    own = out_ref.shape[0] - 1
    lanes, tile = out_ref.shape[1:]
    bins, snaps = m_ref.shape[:2]
    for f in range(bins):
        for b in range(own):
            out_ref[b, f * snaps : (f + 1) * snaps] = m_ref[f, :, b * tile : (b + 1) * tile].astype(BF16)
    lane = lax.broadcasted_iota(jnp.int32, (lanes, tile), 1)
    note = jnp.full((lanes, tile), -1, jnp.int32)
    for s in range(pattern_ref.shape[1]):
        note = jnp.where((lane == s) & (s < count_ref[0]), pattern_ref[0, s], note)
    out_ref[own] = note.astype(F32).astype(BF16)


def shrink(moved, energies, step, penalty):
    energy = energies[0]
    for other in energies[1:]:
        energy = energy + other
    return moved * jnp.maximum(0.0, 1.0 - step * penalty / jnp.sqrt(energy + 1e-6))


def next_kernel(groups, snaps, *refs):
    pattern_ref, step_ref, moved_ref = refs[:3]
    energy_refs = refs[3 : 3 + groups]
    penalty_ref, a_ref, cur_ref, c_ref, cb_ref, xm_ref = refs[3 + groups :]
    slots, bins = a_ref.shape[0], a_ref.shape[1]
    value = shrink(moved_ref[...], [e[...] for e in energy_refs], step_ref[0], penalty_ref[...])
    cur_ref[...] = value
    for f, part in enumerate(masked_rows(value, bins, snaps)):
        xm_ref[f] = part
    for s in range(slots):
        forward_slot(s, pattern_ref, xm_ref, a_ref, c_ref, cb_ref)


def last_kernel(groups, snaps, *refs):
    step_ref, moved_ref = refs[:2]
    energy_refs = refs[2 : 2 + groups]
    penalty_ref, out_ref = refs[2 + groups :]
    value = shrink(moved_ref[...], [e[...] for e in energy_refs], step_ref[0], penalty_ref[...])
    for f in range(out_ref.shape[0]):
        out_ref[f] = value[f * snaps : (f + 1) * snaps]


def backward(live, pattern_ref, step_ref, a_ref, cur_ref, moved_ref, energy_ref, r_ref, canon, acc_ref, snaps):
    slots, bins, tile = a_ref.shape[0], a_ref.shape[1], a_ref.shape[-1]
    acc_ref[...] = jnp.zeros_like(acc_ref)
    for s in range(slots):

        @pl.when(s < live)
        def _():
            parts = masked_rows(r_ref[canon[s]], bins, snaps)
            lhs = jnp.concatenate(parts, axis=1)
            start = column(pattern_ref, s, acc_ref.shape[-1], tile)
            acc_ref[:, pl.ds(start, tile)] += jnp.dot(
                lhs, a_ref[s].reshape(bins * tile, tile), preferred_element_type=F32
            )

    moved = cur_ref[...] - step_ref[0] * acc_ref[...]
    moved_ref[...] = moved
    energy_ref[...] = jnp.sum(moved * moved, axis=0, keepdims=True)


def back_kernel(first, direct, n_recv, n_meas, own, snaps, *refs):
    refs = list(refs)

    def take_refs(n):
        taken, refs[:] = refs[:n], refs[n:]
        return taken

    pattern_ref, count_ref, step_ref, me_ref = take_refs(4)
    learn = direct and first
    if not learn:
        (table_ref,) = take_refs(1)
    c_ref, a_ref, cur_ref = take_refs(3)
    recv_refs = take_refs(n_recv)
    meas_refs = take_refs(n_meas)
    moved_ref, energy_ref = take_refs(2)
    (sel_ref,) = take_refs(1) if first else meas_refs
    if learn:
        (table_ref,) = take_refs(1)
    r_ref, acc_ref, inv, canon = take_refs(4)
    slots = a_ref.shape[0]
    live = count_ref[0]
    me = me_ref[0]
    if learn:
        note_ref, sem = refs
        for k in range(n_meas):
            note_ref[k : k + 1] = meas_refs[k][own, 0:1, :128].astype(F32).astype(jnp.int32)
        copy = pltpu.make_async_copy(note_ref, table_ref, sem)
        copy.start()
    blocks = inv.shape[0]

    def clear(b, _):
        inv[b] = -1
        return 0

    lax.fori_loop(0, blocks, clear, 0, unroll=8)
    for s in range(slots):
        row = pattern_ref[0, s]
        held = inv[row]
        fresh = held < 0
        canon[s] = jnp.where(fresh, s, held)

        @pl.when((s < live) & fresh)
        def _():
            inv[row] = s
            r_ref[s] = c_ref[s] if first else c_ref[s] - sel_ref[s]

        @pl.when((s < live) & jnp.logical_not(fresh))
        def _():
            r_ref[held] += c_ref[s]

    if first:
        for k, ref in enumerate(meas_refs):
            start = lax.bitwise_xor(me, k) * own if direct else 0

            def take(t, _, ref=ref, start=start):
                slot = inv[start + t]

                @pl.when(slot >= 0)
                def _():
                    value = ref[t].astype(F32)
                    sel_ref[slot] = value
                    r_ref[slot] -= value

                return 0

            lax.fori_loop(0, own, take, 0, unroll=min(own, 8))
    if learn:
        copy.wait()

    for k, ref in enumerate(recv_refs):

        def add(t, _, ref=ref, k=k):
            if direct:
                row = table_ref[k + 1, t]
            else:
                row = jnp.where(t // slots == me, -1, table_ref[t])
            slot = jnp.where(row >= 0, inv[jnp.maximum(row, 0)], -1)

            @pl.when(slot >= 0)
            def _():
                r_ref[slot] += ref[t].astype(F32)

            return 0

        lax.fori_loop(0, ref.shape[0], add, 0, unroll=slots)
    backward(live, pattern_ref, step_ref, a_ref, cur_ref, moved_ref, energy_ref, r_ref, canon, acc_ref, snaps)


def body(count_scan, count_bin, tile_blocks, tile_pattern, tile_count, initial_map, measured, step_size, penalty):
    slots, bins, tile, _ = tile_blocks.shape
    snaps, points = initial_map.shape[1:]
    lanes = bins * snaps
    sensors_dev = measured.shape[2]
    blocks = sensors_dev * count_scan // tile
    me = lax.axis_index("scan").astype(jnp.int32)[None]
    shape = jax.ShapeDtypeStruct
    grant = pltpu.CompilerParams(vmem_limit_bytes=12 << 20)
    big = pltpu.CompilerParams(vmem_limit_bytes=24 << 20)
    direct = (
        count_scan <= 8
        and count_scan & (count_scan - 1) == 0
        and sensors_dev % tile == 0
        and blocks <= 256
        and slots <= 128
    )

    def spread(value):
        if direct:
            return [
                lax.ppermute(value, "scan", [(i, i ^ k) for i in range(count_scan)])
                for k in range(1, count_scan)
            ]
        return [lax.all_gather(value, "scan", axis=0, tiled=True)]

    if direct:
        own = sensors_dev // tile
        sent = pl.pallas_call(
            send_kernel,
            out_shape=shape((own + 1, lanes, tile), BF16),
            in_specs=[smem(), smem(), vmem()],
            out_specs=vmem(),
            compiler_params=grant,
        )(tile_pattern, tile_count, measured)
        meas = [sent] + spread(sent)
        table = None
    else:
        full = lax.all_gather(measured.astype(BF16), "scan", axis=2, tiled=True)
        meas = [full.reshape(lanes, blocks, tile).transpose(1, 0, 2)]
        own = blocks
        rows = jnp.where(jnp.arange(slots, dtype=jnp.int32) < tile_count[0], tile_pattern[0], -1)
        table = lax.all_gather(rows, "scan", axis=0, tiled=True)

    current, contrib, rounded = pl.pallas_call(
        first_kernel,
        out_shape=(
            shape((lanes, points), F32),
            shape((slots, lanes, tile), F32),
            shape((slots, lanes, tile), BF16),
        ),
        in_specs=[smem(), vmem(), vmem()],
        out_specs=(vmem(),) * 3,
        scratch_shapes=[pltpu.VMEM((bins, lanes, points), BF16)],
        compiler_params=grant,
    )(tile_pattern, initial_map, tile_blocks)

    chosen = None
    pen = penalty.reshape(1, points)
    for iteration in range(ITERS):
        first = iteration == 0
        received = spread(rounded)
        given = meas if first else [chosen]
        learn = direct and first
        outs = [shape((lanes, points), F32), shape((1, points), F32)]
        out_specs = [vmem(), vmem()]
        scratch = [
            pltpu.VMEM((slots, lanes, tile), F32),
            pltpu.VMEM((lanes, points), F32),
            pltpu.SMEM((blocks,), jnp.int32),
            pltpu.SMEM((slots,), jnp.int32),
        ]
        if first:
            outs.append(shape((slots, lanes, tile), F32))
            out_specs.append(vmem())
        if learn:
            outs.append(shape((count_scan, 128), jnp.int32))
            out_specs.append(smem())
            scratch += [pltpu.VMEM((count_scan, 128), jnp.int32), pltpu.SemaphoreType.DMA]
        tables = [] if learn else [table]
        results = pl.pallas_call(
            functools.partial(back_kernel, first, direct, len(received), len(given), own, snaps),
            out_shape=tuple(outs),
            in_specs=[smem()] * (4 + len(tables)) + [vmem()] * (3 + len(received) + len(given)),
            out_specs=tuple(out_specs),
            scratch_shapes=scratch,
            compiler_params=big,
        )(tile_pattern, tile_count, step_size, me, *tables, contrib, tile_blocks, current, *received, *given)
        moved, energy = results[:2]
        if first:
            chosen = results[2]
        if learn:
            table = results[3]
        energies = [energy] + [
            lax.ppermute(energy, "bin", [(i, (i + k) % count_bin) for i in range(count_bin)])
            for k in range(1, count_bin)
        ]
        if iteration < ITERS - 1:
            current, contrib, rounded = pl.pallas_call(
                functools.partial(next_kernel, count_bin, snaps),
                out_shape=(
                    shape((lanes, points), F32),
                    shape((slots, lanes, tile), F32),
                    shape((slots, lanes, tile), BF16),
                ),
                in_specs=[smem(), smem()] + [vmem()] * (3 + count_bin),
                out_specs=(vmem(),) * 3,
                scratch_shapes=[pltpu.VMEM((bins, lanes, points), BF16)],
                compiler_params=grant,
            )(tile_pattern, step_size, moved, *energies, pen, tile_blocks)
    return pl.pallas_call(
        functools.partial(last_kernel, count_bin, snaps),
        out_shape=shape(initial_map.shape, F32),
        in_specs=[smem()] + [vmem()] * (2 + count_bin),
        out_specs=vmem(),
        compiler_params=grant,
    )(step_size, moved, *energies, pen)


def solution(mesh):
    in_specs = (
        P("scan", "bin", None, None),
        P(None, "scan"),
        P("scan"),
        P("bin", None, "scan"),
        P("bin", None, "scan"),
        P(),
        P("scan"),
    )
    run = functools.partial(body, mesh.shape["scan"], mesh.shape["bin"])
    return jax.shard_map(run, mesh=mesh, in_specs=in_specs, out_specs=P("bin", None, "scan"), check_vma=False)
```

```python
import functools

import jax
import jax.numpy as jnp
from jax import lax
from jax.experimental import pallas as pl
from jax.experimental.pallas import tpu as pltpu
from jax.sharding import PartitionSpec as P

ITERS = 2
BITS = 14
ROWS_AT = 128
PRODUCT_AT = 64
F32 = jnp.float32
BF16 = jnp.bfloat16
I32 = jnp.int32
I16 = jnp.int16


def vmem():
    return pl.BlockSpec(memory_space=pltpu.VMEM)


def smem():
    return pl.BlockSpec(memory_space=pltpu.SMEM)


def hbm():
    return pl.BlockSpec(memory_space=pltpu.HBM)


def in_hbm(value):
    return pltpu.with_memory_space_constraint(value, pltpu.HBM)


def taker(refs):
    refs = list(refs)

    def take(n):
        taken, refs[:] = refs[:n], refs[n:]
        return taken

    return take


class Info:
    def __init__(self, ref, slots):
        self.ref, self.slots = ref, slots

    @staticmethod
    def size(slots):
        return 3 * slots + 2

    def row(self, s):
        return self.ref[s]

    def col(self, s):
        return self.ref[self.slots + s]

    def first(self, s):
        return self.ref[2 * self.slots + s]

    def shared(self):
        return self.ref[3 * self.slots]

    def live(self):
        return self.ref[3 * self.slots + 1]

    def fill(self, pattern_ref, count_ref, columns):
        slots, live = self.slots, count_ref[0]
        rows = [pattern_ref[0, s] for s in range(slots)]
        flag = jnp.int32(0)
        for s in range(slots):
            first = jnp.int32(s)
            for t in range(s - 1, -1, -1):
                first = jnp.where((rows[t] == rows[s]) & (s < live), t, first)
            self.ref[s] = rows[s]
            self.ref[slots + s] = lax.rem(pattern_ref[1, s], columns)
            self.ref[2 * slots + s] = first
            flag = flag | (first < s).astype(I32)
        self.ref[3 * slots] = flag
        self.ref[3 * slots + 1] = live


def start_tiles(a_hbm, a_ref, sems):
    copies = [pltpu.make_async_copy(a_hbm.at[s], a_ref.at[s], sems.at[s]) for s in range(a_ref.shape[0])]
    for copy in copies:
        copy.start()
    return copies


def masked_rows(value, bins, snaps):
    row = lax.broadcasted_iota(I32, value.shape, 0) // snaps
    return [jnp.where(row == f, value, 0.0).astype(BF16) for f in range(bins)]


def encode(value):
    top = jnp.max(jnp.abs(value), axis=1, keepdims=True)
    power = jnp.clip(jnp.ceil(jnp.log2(jnp.maximum(top, 1e-30))), -100.0, 127.0)
    code = jnp.clip(jnp.round(value * jnp.exp2(BITS - power)), -32767.0, 32767.0)
    return code.astype(I32).astype(I16), power.astype(I32)


def decode(code, note, lane, at):
    power = jnp.sum(jnp.where(lane == at, note, 0.0), axis=1, keepdims=True)
    return code.astype(I32).astype(F32) * jnp.exp2(power - BITS)


def forward(value, snaps, info, waits, xm_ref, a_ref, c_ref):
    slots, bins, tile = a_ref.shape[0], a_ref.shape[1], a_ref.shape[-1]
    for f, part in enumerate(masked_rows(value, bins, snaps)):
        xm_ref[f] = part
    for s in range(slots):
        for copy in waits.get(s, ()):
            copy.wait()
        start = pl.multiple_of(info.col(s) * tile, tile)
        total = None
        for f in range(bins):
            part = lax.dot_general(
                xm_ref[f, :, pl.ds(start, tile)],
                a_ref[s, f],
                (((1,), (1,)), ((), ())),
                preferred_element_type=F32,
            )
            total = part if total is None else total + part
        c_ref[s] = total

    @pl.when(info.shared() > 0)
    def _():
        for s in range(1, slots):
            first = info.first(s)

            @pl.when(first < s)
            def _():
                c_ref[first] += c_ref[s]


def start_kernel(coded, columns, count_ref, pattern_hbm, x_hbm, m_hbm, a_hbm, *refs):
    cur_ref, c_ref, out_ref, info_ref, pattern_ref, x_ref, m_ref, a_ref, xm_ref, small, sems = refs
    slots = a_ref.shape[0]
    bins, snaps = x_ref.shape[:2]
    loads = [
        pltpu.make_async_copy(source, target, small.at[i])
        for i, (source, target) in enumerate(
            [(pattern_hbm, pattern_ref), (x_hbm, x_ref), (m_hbm, m_ref)]
        )
    ]
    for load in loads:
        load.start()
    copies = start_tiles(a_hbm, a_ref, sems)
    waits = {s: copies[s : s + 2] for s in range(0, slots, 2)}
    loads[0].wait()
    info = Info(info_ref, slots)
    info.fill(pattern_ref, count_ref, columns)
    loads[1].wait()
    value = jnp.concatenate([x_ref[f] for f in range(bins)], axis=0)
    cur_ref[...] = value
    loads[2].wait()
    lanes, tile = out_ref.shape[1:]
    if coded:
        own = out_ref.shape[0] - slots - 1
        lane = lax.broadcasted_iota(I32, (lanes, tile), 1)
        note = jnp.full((lanes, tile), -1, I32)
        for b in range(own):
            code, power = encode(
                jnp.concatenate([m_ref[f, :, b * tile : (b + 1) * tile] for f in range(bins)], axis=0)
            )
            out_ref[b] = code
            note = jnp.where(lane == b, power, note)
        for s in range(slots):
            keep = (s < info.live()) & (info.first(s) == s)
            note = jnp.where((lane == ROWS_AT + s) & keep, info.row(s), note)
    forward(value, snaps, info, waits, xm_ref, a_ref, c_ref)
    for s in range(slots):
        if coded:
            code, power = encode(c_ref[s])
            out_ref[own + s] = code
            note = jnp.where(lane == PRODUCT_AT + s, power, note)
        else:
            out_ref[s] = c_ref[s].astype(BF16)
    if coded:
        out_ref[own + slots] = note.astype(I16)


def shrink(moved, energies, step, penalty):
    energy = energies[0]
    for other in energies[1:]:
        energy = energy + other
    return moved * jnp.maximum(0.0, 1.0 - step * penalty / jnp.sqrt(energy + 1e-6))


def next_kernel(groups, snaps, *refs):
    take = taker(refs)
    info_ref, step_ref, moved_ref = take(3)
    energy_refs = take(groups)
    penalty_ref, a_ref, cur_ref, c_ref, out_ref, xm_ref = take(6)
    slots = a_ref.shape[0]
    value = shrink(moved_ref[...], [e[...] for e in energy_refs], step_ref[0], penalty_ref[...])
    cur_ref[...] = value
    forward(value, snaps, Info(info_ref, slots), {}, xm_ref, a_ref, c_ref)
    for s in range(slots):
        out_ref[s] = c_ref[s].astype(BF16)


def last_kernel(groups, snaps, *refs):
    take = taker(refs)
    step_ref, moved_ref = take(2)
    energy_refs = take(groups)
    penalty_ref, out_ref = take(2)
    value = shrink(moved_ref[...], [e[...] for e in energy_refs], step_ref[0], penalty_ref[...])
    for f in range(out_ref.shape[0]):
        out_ref[f] = value[f * snaps : (f + 1) * snaps]


def find_common(info, coded, count, slots, me, rows, order_ref, table, sem, entries_ref):
    other = lax.broadcasted_iota(I32, rows.shape, 0)
    if coded:
        other = other ^ me
    found = jnp.full(rows.shape, -1, I32)
    for s in range(slots):
        row = jnp.where((s < info.live()) & (info.first(s) == s), info.row(s), -2)
        found = jnp.where(rows == row, s, found)
    order_ref[...] = jnp.where(other == me, -1, found)
    copy = pltpu.make_async_copy(order_ref, table, sem)
    copy.start()

    def finish():
        copy.wait()

        def one(k, number):
            entries_ref[k] = number
            for t in range(slots):
                slot = table[k, t]
                entries_ref[number] = (t if coded else k * slots + t) * 64 + slot
                number = number + (slot >= 0).astype(I32)
            return number

        entries_ref[count] = lax.fori_loop(0, count, one, jnp.int32(count + 1))

    return finish


def gradient(info, columns, snaps, a_ref, r_ref):
    slots, bins, tile = a_ref.shape[0], a_ref.shape[1], a_ref.shape[-1]
    sums = [jnp.zeros((bins * snaps, tile), F32) for _ in range(columns)]
    for s in range(slots):
        value = jnp.where(s < info.live(), r_ref[info.first(s)], 0.0)
        lhs = jnp.concatenate(masked_rows(value, bins, snaps), axis=1)
        part = jnp.dot(lhs, a_ref[s].reshape(bins * tile, tile), preferred_element_type=F32)
        sums = [total + jnp.where(info.col(s) == i, part, 0.0) for i, total in enumerate(sums)]
    return jnp.concatenate(sums, axis=1)


def finish_step(cur_ref, step_ref, grad, moved_ref, energy_ref):
    moved = cur_ref[...] - step_ref[0] * grad
    moved_ref[...] = moved
    energy_ref[...] = jnp.sum(moved * moved, axis=0, keepdims=True)


def first_back_kernel(coded, count, snaps, *refs):
    take = taker(refs)
    info_ref, step_ref, me_ref, c_ref, cur_ref, a_hbm = take(6)
    arrived = take(count) if coded else take(3)
    moved_ref, energy_ref, sel_ref, a_ref, entries_ref, r_ref = take(6)
    rows_ref, order_ref, table, sem, sems = take(5)
    slots, tile = a_ref.shape[0], a_ref.shape[-1]
    info = Info(info_ref, slots)
    me = me_ref[0]
    copies = start_tiles(a_hbm, a_ref, sems)
    if coded:
        stack_ref, stack_sems = take(2)
        last = arrived[0].shape[0] - 1
        own = last - slots
        moves = [
            pltpu.make_async_copy(ref.at[pl.ds(0, own)], stack_ref.at[pl.ds(k * own, own)], stack_sems.at[k])
            for k, ref in enumerate(arrived)
        ] + [
            pltpu.make_async_copy(ref.at[pl.ds(last, 1)], stack_ref.at[pl.ds(count * own + k, 1)], stack_sems.at[count + k])
            for k, ref in enumerate(arrived)
        ]
        for move in moves:
            move.start()
        for k, ref in enumerate(arrived):
            rows_ref[k : k + 1] = ref[last, 0:1, ROWS_AT : ROWS_AT + 128].astype(I32)
    else:
        full_ref, table_ref, recv_ref = arrived
        rows_ref[...] = table_ref[...]
    finish = find_common(info, coded, count, slots, me, rows_ref[...], order_ref, table, sem, entries_ref)
    if coded:
        lane = lax.broadcasted_iota(I32, stack_ref.shape[1:], 1)
        for move in moves:
            move.wait()
        for s in range(slots):
            k = lax.bitwise_xor(me, lax.div(info.row(s), own))
            at = lax.rem(info.row(s), own)
            note = stack_ref[count * own + k].astype(I32).astype(F32)
            sel_ref[s] = decode(stack_ref[k * own + at], note, lane, at)
    else:
        for s in range(slots):
            sel_ref[s] = full_ref[info.row(s)]
    for s in range(slots):
        r_ref[s] = c_ref[s] - sel_ref[s]
    finish()
    if coded:
        for k in range(1, count):

            def add(i, _, k=k):
                at, slot = lax.shift_right_logical(entries_ref[i], 6), entries_ref[i] & 63
                note = arrived[k][last].astype(I32).astype(F32)
                r_ref[slot] += decode(arrived[k][own + at], note, lane, PRODUCT_AT + at)
                return 0

            lax.fori_loop(entries_ref[k], entries_ref[k + 1], add, 0)
    else:
        add_blocks(entries_ref, 0, count, recv_ref, r_ref)
    for copy in copies:
        copy.wait()
    grad = gradient(info, cur_ref.shape[1] // tile, snaps, a_ref, r_ref)
    finish_step(cur_ref, step_ref, grad, moved_ref, energy_ref)


def add_blocks(entries_ref, low, high, ref, r_ref):
    def add(i, _):
        at, slot = lax.shift_right_logical(entries_ref[i], 6), entries_ref[i] & 63
        r_ref[slot] += ref[at].astype(F32)
        return 0

    lax.fori_loop(entries_ref[low], entries_ref[high], add, 0)


def back_kernel(coded, count, snaps, *refs):
    take = taker(refs)
    info_ref, step_ref, entries_ref, c_ref, cur_ref, sel_ref, a_ref = take(7)
    arrived = take(count - 1 if coded else 1)
    moved_ref, energy_ref, r_ref = take(3)
    slots, tile = a_ref.shape[0], a_ref.shape[-1]
    info = Info(info_ref, slots)
    for s in range(slots):
        r_ref[s] = c_ref[s] - sel_ref[s]
    if coded:
        for k, ref in enumerate(arrived):
            add_blocks(entries_ref, k + 1, k + 2, ref, r_ref)
    else:
        add_blocks(entries_ref, 0, count, arrived[0], r_ref)
    grad = gradient(info, cur_ref.shape[1] // tile, snaps, a_ref, r_ref)
    finish_step(cur_ref, step_ref, grad, moved_ref, energy_ref)


def body(count, groups, tile_blocks, tile_pattern, tile_count, initial_map, measured, step_size, penalty):
    slots, bins, tile, _ = tile_blocks.shape
    snaps, points = initial_map.shape[1:]
    lanes = bins * snaps
    sensors_dev = measured.shape[2]
    blocks = sensors_dev * count // tile
    columns = points // tile
    own = sensors_dev // tile
    me = lax.axis_index("scan").astype(I32)[None]
    shape = jax.ShapeDtypeStruct
    grant = pltpu.CompilerParams(vmem_limit_bytes=20 << 20)
    coded = (
        count <= 8
        and count & (count - 1) == 0
        and sensors_dev % tile == 0
        and own <= PRODUCT_AT
        and slots < 64
        and tile >= ROWS_AT + 128
    )
    map_shape = shape((lanes, points), F32)
    slot_shape = shape((slots, lanes, tile), F32)
    sent_shape = shape((slots, lanes, tile), BF16)
    tile_shape = shape(tile_blocks.shape, BF16)
    masked = pltpu.VMEM((bins, lanes, points), BF16)
    tile_sems = pltpu.SemaphoreType.DMA((slots,))

    def swap(value, k):
        return lax.ppermute(value, "scan", [(i, i ^ k) for i in range(count)])

    def spread(value):
        if not coded:
            return [lax.all_gather(value, "scan", axis=0, tiled=True)]
        got = {k: swap(value, k) for k in [*range(4, count, 2), *range(2, min(count, 4), 2)]}
        got[1] = swap(value, 1)
        for k in range(2, count, 2):
            got[k + 1] = swap(got[k], 1)
        return [got[k] for k in range(1, count)]

    current, contrib, sent, info = pl.pallas_call(
        functools.partial(start_kernel, coded, columns),
        out_shape=(
            map_shape,
            slot_shape,
            shape((own + slots + 1, lanes, tile), I16) if coded else sent_shape,
            shape((Info.size(slots),), I32),
        ),
        in_specs=[smem()] + [hbm()] * 4,
        out_specs=(vmem(), vmem(), vmem(), smem()),
        scratch_shapes=[
            pltpu.SMEM(tile_pattern.shape, I32),
            pltpu.VMEM(initial_map.shape, F32),
            pltpu.VMEM(measured.shape, F32),
            pltpu.VMEM(tile_blocks.shape, BF16),
            masked,
            pltpu.SemaphoreType.DMA((3,)),
            tile_sems,
        ],
        compiler_params=grant,
    )(tile_count, in_hbm(tile_pattern), in_hbm(initial_map), in_hbm(measured), in_hbm(tile_blocks))

    if coded:
        given = [sent] + spread(sent)
    else:
        full = lax.all_gather(measured, "scan", axis=2, tiled=True)
        order = jnp.arange(slots, dtype=I32)
        keep = (order < tile_count[0]) & (info[2 * slots : 3 * slots] == order)
        rows = jnp.pad(jnp.where(keep, tile_pattern[0], -1), (0, 128 - slots), constant_values=-1)
        given = [
            full.reshape(lanes, blocks, tile).transpose(1, 0, 2),
            lax.all_gather(rows[None], "scan", axis=0, tiled=True),
        ] + spread(sent)

    pen = penalty.reshape(1, points)
    energy_shape = shape((1, points), F32)
    for iteration in range(ITERS):
        if iteration == 0:
            scratch = [
                pltpu.VMEM(slot_shape.shape, F32),
                pltpu.VMEM((count, 128), I32),
                pltpu.VMEM((count, 128), I32),
                pltpu.SMEM((count, 128), I32),
                pltpu.SemaphoreType.DMA,
                tile_sems,
            ]
            if coded:
                scratch.append(pltpu.VMEM((count * (own + 1), lanes, tile), I16))
                scratch.append(pltpu.SemaphoreType.DMA((2 * count,)))
            moved, energy, chosen, held, entries = pl.pallas_call(
                functools.partial(first_back_kernel, coded, count, snaps),
                out_shape=(
                    map_shape, energy_shape, slot_shape, tile_shape,
                    shape((count + 2 + count * slots,), I32),
                ),
                in_specs=[smem()] * 3 + [vmem(), vmem(), hbm()] + [vmem()] * len(given),
                out_specs=(vmem(),) * 4 + (smem(),),
                scratch_shapes=scratch,
                compiler_params=grant,
            )(info, step_size, me, contrib, current, in_hbm(tile_blocks), *given)
        else:
            received = spread(sent)
            moved, energy = pl.pallas_call(
                functools.partial(back_kernel, coded, count, snaps),
                out_shape=(map_shape, energy_shape),
                in_specs=[smem()] * 3 + [vmem()] * (4 + len(received)),
                out_specs=(vmem(),) * 2,
                scratch_shapes=[pltpu.VMEM(slot_shape.shape, F32)],
                compiler_params=grant,
            )(info, step_size, entries, contrib, current, chosen, held, *received)
        energies = [energy] + [
            lax.ppermute(energy, "bin", [(i, (i + k) % groups) for i in range(groups)])
            for k in range(1, groups)
        ]
        if iteration < ITERS - 1:
            current, contrib, sent = pl.pallas_call(
                functools.partial(next_kernel, groups, snaps),
                out_shape=(map_shape, slot_shape, sent_shape),
                in_specs=[smem()] * 2 + [vmem()] * (3 + groups),
                out_specs=(vmem(),) * 3,
                scratch_shapes=[masked],
                compiler_params=grant,
            )(info, step_size, moved, *energies, pen, held)
    return pl.pallas_call(
        functools.partial(last_kernel, groups, snaps),
        out_shape=shape(initial_map.shape, F32),
        in_specs=[smem()] + [vmem()] * (2 + groups),
        out_specs=vmem(),
        compiler_params=grant,
    )(step_size, moved, *energies, pen)


def solution(mesh):
    in_specs = (
        P("scan", "bin", None, None),
        P(None, "scan"),
        P("scan"),
        P("bin", None, "scan"),
        P("bin", None, "scan"),
        P(),
        P("scan"),
    )
    run = functools.partial(body, mesh.shape["scan"], mesh.shape["bin"])
    return jax.shard_map(run, mesh=mesh, in_specs=in_specs, out_specs=P("bin", None, "scan"), check_vma=False)
```

```python
import functools

import jax
import jax.numpy as jnp
from jax import lax
from jax.experimental import pallas as pl
from jax.experimental.pallas import tpu as pltpu
from jax.sharding import PartitionSpec as P

ITERS = 2
BITS = 14
ROWS_AT = 128
PRODUCT_AT = 64
F32 = jnp.float32
BF16 = jnp.bfloat16
I32 = jnp.int32
I16 = jnp.int16


def vmem():
    return pl.BlockSpec(memory_space=pltpu.VMEM)


def smem():
    return pl.BlockSpec(memory_space=pltpu.SMEM)


def hbm():
    return pl.BlockSpec(memory_space=pltpu.HBM)


def in_hbm(value):
    return pltpu.with_memory_space_constraint(value, pltpu.HBM)


def taker(refs):
    refs = list(refs)

    def take(n):
        taken, refs[:] = refs[:n], refs[n:]
        return taken

    return take


class Info:
    def __init__(self, ref, slots):
        self.ref, self.slots = ref, slots

    @staticmethod
    def size(slots):
        return 3 * slots + 2

    def row(self, s):
        return self.ref[s]

    def col(self, s):
        return self.ref[self.slots + s]

    def first(self, s):
        return self.ref[2 * self.slots + s]

    def shared(self):
        return self.ref[3 * self.slots]

    def live(self):
        return self.ref[3 * self.slots + 1]

    def fill(self, pattern_ref, count_ref, columns):
        slots, live = self.slots, count_ref[0]
        rows = [pattern_ref[0, s] for s in range(slots)]
        flag = jnp.int32(0)
        for s in range(slots):
            first = jnp.int32(s)
            for t in range(s - 1, -1, -1):
                first = jnp.where((rows[t] == rows[s]) & (s < live), t, first)
            self.ref[s] = rows[s]
            self.ref[slots + s] = lax.rem(pattern_ref[1, s], columns)
            self.ref[2 * slots + s] = first
            flag = flag | (first < s).astype(I32)
        self.ref[3 * slots] = flag
        self.ref[3 * slots + 1] = live


def start_tiles(a_hbm, a_ref, sems, low, high):
    copies = [pltpu.make_async_copy(a_hbm.at[s], a_ref.at[s], sems.at[s]) for s in range(low, high)]
    for copy in copies:
        copy.start()
    return copies


def masked_rows(value, bins, snaps):
    row = lax.broadcasted_iota(I32, value.shape, 0) // snaps
    return [jnp.where(row == f, value, 0.0).astype(BF16) for f in range(bins)]


def encode(value):
    top = jnp.max(jnp.abs(value), axis=1, keepdims=True)
    power = jnp.clip(jnp.ceil(jnp.log2(jnp.maximum(top, 1e-30))), -100.0, 127.0)
    code = jnp.clip(jnp.round(value * jnp.exp2(BITS - power)), -32767.0, 32767.0)
    return code.astype(I32).astype(I16), power.astype(I32)


def decode(code, note, lane, at):
    power = jnp.sum(jnp.where(lane == at, note, 0.0), axis=1, keepdims=True)
    return code.astype(I32).astype(F32) * jnp.exp2(power - BITS)


def forward(value, snaps, info, waits, xm_ref, a_ref, c_ref):
    slots, bins, tile = a_ref.shape[0], a_ref.shape[1], a_ref.shape[-1]
    for f, part in enumerate(masked_rows(value, bins, snaps)):
        xm_ref[f] = part
    for s in range(slots):
        for copy in waits.get(s, ()):
            copy.wait()
        start = pl.multiple_of(info.col(s) * tile, tile)
        total = None
        for f in range(bins):
            part = lax.dot_general(
                xm_ref[f, :, pl.ds(start, tile)],
                a_ref[s, f],
                (((1,), (1,)), ((), ())),
                preferred_element_type=F32,
            )
            total = part if total is None else total + part
        c_ref[s] = total

    @pl.when(info.shared() > 0)
    def _():
        for s in range(1, slots):
            first = info.first(s)

            @pl.when(first < s)
            def _():
                c_ref[first] += c_ref[s]


def start_kernel(coded, columns, count_ref, pattern_hbm, x_hbm, m_hbm, a_hbm, *refs):
    cur_ref, c_ref, out_ref, info_ref, pattern_ref, x_ref, m_ref, a_ref, xm_ref, small, sems = refs
    slots = a_ref.shape[0]
    bins, snaps = x_ref.shape[:2]
    loads = [
        pltpu.make_async_copy(source, target, small.at[i])
        for i, (source, target) in enumerate(
            [(pattern_hbm, pattern_ref), (x_hbm, x_ref), (m_hbm, m_ref)]
        )
    ]
    for load in loads:
        load.start()
    copies = start_tiles(a_hbm, a_ref, sems, 0, slots * 3 // 4)
    loads[0].wait()
    info = Info(info_ref, slots)
    info.fill(pattern_ref, count_ref, columns)
    loads[1].wait()
    value = jnp.concatenate([x_ref[f] for f in range(bins)], axis=0)
    cur_ref[...] = value
    copies += start_tiles(a_hbm, a_ref, sems, slots * 3 // 4, slots)
    waits = {0: copies[: slots * 3 // 4], slots * 3 // 4: copies[slots * 3 // 4 :]}
    loads[2].wait()
    lanes, tile = out_ref.shape[1:]
    if coded:
        own = out_ref.shape[0] - slots - 1
        lane = lax.broadcasted_iota(I32, (lanes, tile), 1)
        note = jnp.full((lanes, tile), -1, I32)
        for b in range(own):
            code, power = encode(
                jnp.concatenate([m_ref[f, :, b * tile : (b + 1) * tile] for f in range(bins)], axis=0)
            )
            out_ref[b] = code
            note = jnp.where(lane == b, power, note)
        for s in range(slots):
            keep = (s < info.live()) & (info.first(s) == s)
            note = jnp.where((lane == ROWS_AT + s) & keep, info.row(s), note)
    forward(value, snaps, info, waits, xm_ref, a_ref, c_ref)
    for s in range(slots):
        if coded:
            code, power = encode(c_ref[s])
            out_ref[own + s] = code
            note = jnp.where(lane == PRODUCT_AT + s, power, note)
        else:
            out_ref[s] = c_ref[s].astype(BF16)
    if coded:
        out_ref[own + slots] = note.astype(I16)


def shrink(moved, energies, step, penalty):
    energy = energies[0]
    for other in energies[1:]:
        energy = energy + other
    return moved * jnp.maximum(0.0, 1.0 - step * penalty / jnp.sqrt(energy + 1e-6))


def next_kernel(groups, snaps, *refs):
    take = taker(refs)
    info_ref, step_ref, moved_ref = take(3)
    energy_refs = take(groups)
    penalty_ref, a_ref, cur_ref, c_ref, out_ref, xm_ref = take(6)
    slots = a_ref.shape[0]
    value = shrink(moved_ref[...], [e[...] for e in energy_refs], step_ref[0], penalty_ref[...])
    cur_ref[...] = value
    forward(value, snaps, Info(info_ref, slots), {}, xm_ref, a_ref, c_ref)
    for s in range(slots):
        out_ref[s] = c_ref[s].astype(BF16)


def last_kernel(groups, snaps, *refs):
    take = taker(refs)
    step_ref, moved_ref = take(2)
    energy_refs = take(groups)
    penalty_ref, out_ref = take(2)
    value = shrink(moved_ref[...], [e[...] for e in energy_refs], step_ref[0], penalty_ref[...])
    for f in range(out_ref.shape[0]):
        out_ref[f] = value[f * snaps : (f + 1) * snaps]


def find_common(info, steps, slots, me, rows, order_ref, table, sem, entries_ref):
    sources = rows.shape[0]
    other = lax.broadcasted_iota(I32, rows.shape, 0)
    if steps is not None:
        far = jnp.zeros(rows.shape, I32)
        for i, k in enumerate(steps):
            far = jnp.where(other == i, k, far)
        other = far ^ me
    found = jnp.full(rows.shape, -1, I32)
    for s in range(slots):
        row = jnp.where((s < info.live()) & (info.first(s) == s), info.row(s), -2)
        found = jnp.where(rows == row, s, found)
    order_ref[...] = jnp.where(other == me, -1, found)
    copy = pltpu.make_async_copy(order_ref, table, sem)
    copy.start()

    def finish():
        copy.wait()

        def one(k, number):
            entries_ref[k] = number
            for t in range(slots):
                slot = table[k, t]
                entries_ref[number] = (t if steps is not None else k * slots + t) * 64 + slot
                number = number + (slot >= 0).astype(I32)
            return number

        entries_ref[sources] = lax.fori_loop(0, sources, one, jnp.int32(sources + 1))

    return finish


def gradient(info, columns, snaps, a_ref, r_ref):
    slots, bins, tile = a_ref.shape[0], a_ref.shape[1], a_ref.shape[-1]
    sums = [jnp.zeros((bins * snaps, tile), F32) for _ in range(columns)]
    for s in range(slots):
        value = jnp.where(s < info.live(), r_ref[info.first(s)], 0.0)
        lhs = jnp.concatenate(masked_rows(value, bins, snaps), axis=1)
        part = jnp.dot(lhs, a_ref[s].reshape(bins * tile, tile), preferred_element_type=F32)
        sums = [total + jnp.where(info.col(s) == i, part, 0.0) for i, total in enumerate(sums)]
    return jnp.concatenate(sums, axis=1)


def finish_step(cur_ref, step_ref, grad, moved_ref, energy_ref):
    moved = cur_ref[...] - step_ref[0] * grad
    moved_ref[...] = moved
    energy_ref[...] = jnp.sum(moved * moved, axis=0, keepdims=True)


def take_in(steps, refs, info, me, rows_ref, order_ref, table, sem, entries_ref, sel_ref, r_ref):
    slots = r_ref.shape[0]
    last = refs[0].shape[0] - 1
    own = last - slots
    for i, ref in enumerate(refs):
        rows_ref[i : i + 1] = ref[last, 0:1, ROWS_AT : ROWS_AT + 128].astype(I32)
    finish = find_common(info, steps, slots, me, rows_ref[...], order_ref, table, sem, entries_ref)
    lane = lax.broadcasted_iota(I32, refs[0].shape[1:], 1)
    homes = [lax.bitwise_xor(me, lax.div(info.row(s), own)) for s in range(slots)]
    for k, ref in zip(steps, refs):
        some = homes[0] == k
        for home in homes[1:]:
            some = some | (home == k)

        @pl.when(some)
        def _(k=k, ref=ref):
            note = ref[last].astype(I32).astype(F32)
            for s in range(slots):

                @pl.when(homes[s] == k)
                def _(s=s):
                    at = lax.rem(info.row(s), own)
                    value = decode(ref[at], note, lane, at)
                    sel_ref[s] = value
                    r_ref[s] -= value

    finish()
    for i, ref in enumerate(refs):

        def add(j, _, ref=ref):
            at, slot = lax.shift_right_logical(entries_ref[j], 6), entries_ref[j] & 63
            note = ref[last].astype(I32).astype(F32)
            r_ref[slot] += decode(ref[own + at], note, lane, PRODUCT_AT + at)
            return 0

        lax.fori_loop(entries_ref[i], entries_ref[i + 1], add, 0)


def early_kernel(coded, steps, *refs):
    take = taker(refs)
    info_ref, me_ref, c_ref, a_hbm = take(4)
    arrived = take(len(steps) if coded else 3)
    r_ref, sel_ref, a_ref, entries_ref, rows_ref, order_ref, table, sem, sems = take(9)
    slots = a_ref.shape[0]
    info = Info(info_ref, slots)
    me = me_ref[0]
    copies = start_tiles(a_hbm, a_ref, sems, 0, slots)
    r_ref[...] = c_ref[...]
    sel_ref[...] = jnp.zeros_like(sel_ref)
    if coded:
        take_in(steps, arrived, info, me, rows_ref, order_ref, table, sem, entries_ref, sel_ref, r_ref)
    else:
        full_ref, table_ref, recv_ref = arrived
        finish = find_common(info, None, slots, me, table_ref[...], order_ref, table, sem, entries_ref)
        for s in range(slots):
            sel_ref[s] = full_ref[info.row(s)]
            r_ref[s] -= sel_ref[s]
        finish()
        add_blocks(entries_ref, 0, table_ref.shape[0], recv_ref, r_ref)
    for copy in copies:
        copy.wait()


def late_kernel(steps, snaps, *refs):
    take = taker(refs)
    info_ref, step_ref, me_ref, part_ref, some_ref, cur_ref, a_ref = take(7)
    arrived = take(len(steps))
    moved_ref, energy_ref, sel_ref, entries_ref, r_ref = take(5)
    slots, tile = a_ref.shape[0], a_ref.shape[-1]
    info = Info(info_ref, slots)
    r_ref[...] = part_ref[...]
    sel_ref[...] = some_ref[...]
    if steps:
        rows_ref, order_ref, table, sem = take(4)
        take_in(steps, arrived, info, me_ref[0], rows_ref, order_ref, table, sem, entries_ref, sel_ref, r_ref)
    else:
        entries_ref[0] = 1
    grad = gradient(info, cur_ref.shape[1] // tile, snaps, a_ref, r_ref)
    finish_step(cur_ref, step_ref, grad, moved_ref, energy_ref)


def add_blocks(entries_ref, low, high, ref, r_ref):
    def add(i, _):
        at, slot = lax.shift_right_logical(entries_ref[i], 6), entries_ref[i] & 63
        r_ref[slot] += ref[at].astype(F32)
        return 0

    lax.fori_loop(entries_ref[low], entries_ref[high], add, 0)


def back_kernel(coded, steps, snaps, *refs):
    take = taker(refs)
    info_ref, step_ref = take(2)
    entry_refs = take(len(steps))
    c_ref, cur_ref, sel_ref, a_ref = take(4)
    arrived = dict(enumerate(take(max(k for part in steps for k in part) if coded else 1), 1))
    moved_ref, energy_ref, r_ref = take(3)
    slots, tile = a_ref.shape[0], a_ref.shape[-1]
    info = Info(info_ref, slots)
    for s in range(slots):
        r_ref[s] = c_ref[s] - sel_ref[s]
    if coded:
        for entries_ref, part in zip(entry_refs, steps):
            for i, k in enumerate(part):
                if k:
                    add_blocks(entries_ref, i, i + 1, arrived[k], r_ref)
    else:
        add_blocks(entry_refs[0], 0, arrived[1].shape[0] // slots, arrived[1], r_ref)
    grad = gradient(info, cur_ref.shape[1] // tile, snaps, a_ref, r_ref)
    finish_step(cur_ref, step_ref, grad, moved_ref, energy_ref)


def body(count, groups, tile_blocks, tile_pattern, tile_count, initial_map, measured, step_size, penalty):
    slots, bins, tile, _ = tile_blocks.shape
    snaps, points = initial_map.shape[1:]
    lanes = bins * snaps
    sensors_dev = measured.shape[2]
    blocks = sensors_dev * count // tile
    columns = points // tile
    own = sensors_dev // tile
    me = lax.axis_index("scan").astype(I32)[None]
    shape = jax.ShapeDtypeStruct
    grant = pltpu.CompilerParams(vmem_limit_bytes=20 << 20)
    coded = (
        count <= 8
        and count & (count - 1) == 0
        and sensors_dev % tile == 0
        and own <= PRODUCT_AT
        and slots < 64
        and tile >= ROWS_AT + 128
    )
    map_shape = shape((lanes, points), F32)
    slot_shape = shape((slots, lanes, tile), F32)
    sent_shape = shape((slots, lanes, tile), BF16)
    tile_shape = shape(tile_blocks.shape, BF16)
    masked = pltpu.VMEM((bins, lanes, points), BF16)
    tile_sems = pltpu.SemaphoreType.DMA((slots,))

    def swap(value, k):
        return lax.ppermute(value, "scan", [(i, i ^ k) for i in range(count)])

    def spread(value):
        if not coded:
            return [lax.all_gather(value, "scan", axis=0, tiled=True)]
        got = {k: swap(value, k) for k in [*range(4, count, 2), *range(2, min(count, 4), 2)]}
        got[1] = swap(value, 1)
        for k in range(2, count, 2):
            got[k + 1] = swap(got[k], 1)
        return [got[k] for k in range(1, count)]

    current, contrib, sent, info = pl.pallas_call(
        functools.partial(start_kernel, coded, columns),
        out_shape=(
            map_shape,
            slot_shape,
            shape((own + slots + 1, lanes, tile), I16) if coded else sent_shape,
            shape((Info.size(slots),), I32),
        ),
        in_specs=[smem()] + [hbm()] * 4,
        out_specs=(vmem(), vmem(), vmem(), smem()),
        scratch_shapes=[
            pltpu.SMEM(tile_pattern.shape, I32),
            pltpu.VMEM(initial_map.shape, F32),
            pltpu.VMEM(measured.shape, F32),
            pltpu.VMEM(tile_blocks.shape, BF16),
            masked,
            pltpu.SemaphoreType.DMA((3,)),
            tile_sems,
        ],
        compiler_params=grant,
    )(tile_count, in_hbm(tile_pattern), in_hbm(initial_map), in_hbm(measured), in_hbm(tile_blocks))

    late = list(range(5, count, 2)) if coded else []
    early = [k for k in range(count) if k not in late] if coded else []
    if coded:
        given = [sent] + spread(sent)
        ready, waiting = [given[k] for k in early], [given[k] for k in late]
    else:
        full = lax.all_gather(measured, "scan", axis=2, tiled=True)
        order = jnp.arange(slots, dtype=I32)
        keep = (order < tile_count[0]) & (info[2 * slots : 3 * slots] == order)
        rows = jnp.pad(jnp.where(keep, tile_pattern[0], -1), (0, 128 - slots), constant_values=-1)
        ready = [
            full.reshape(lanes, blocks, tile).transpose(1, 0, 2),
            lax.all_gather(rows[None], "scan", axis=0, tiled=True),
        ] + spread(sent)
        waiting = []

    def plan_scratch(sources):
        return [
            pltpu.VMEM((sources, 128), I32),
            pltpu.VMEM((sources, 128), I32),
            pltpu.SMEM((sources, 128), I32),
            pltpu.SemaphoreType.DMA,
        ]

    def entries_shape(sources):
        return shape((sources + 2 + sources * slots,), I32)

    pen = penalty.reshape(1, points)
    energy_shape = shape((1, points), F32)
    for iteration in range(ITERS):
        if iteration == 0:
            sources = len(early) if coded else count
            partial, some, held, entries = pl.pallas_call(
                functools.partial(early_kernel, coded, early),
                out_shape=(slot_shape, slot_shape, tile_shape, entries_shape(sources)),
                in_specs=[smem()] * 2 + [vmem(), hbm()] + [vmem()] * len(ready),
                out_specs=(vmem(),) * 3 + (smem(),),
                scratch_shapes=plan_scratch(sources) + [tile_sems],
                compiler_params=grant,
            )(info, me, contrib, in_hbm(tile_blocks), *ready)
            moved, energy, chosen, more = pl.pallas_call(
                functools.partial(late_kernel, late, snaps),
                out_shape=(map_shape, energy_shape, slot_shape, entries_shape(len(late))),
                in_specs=[smem()] * 3 + [vmem()] * (4 + len(waiting)),
                out_specs=(vmem(),) * 3 + (smem(),),
                scratch_shapes=[pltpu.VMEM(slot_shape.shape, F32)] + (plan_scratch(len(late)) if late else []),
                compiler_params=grant,
            )(info, step_size, me, partial, some, current, held, *waiting)
        else:
            received = spread(sent)
            moved, energy = pl.pallas_call(
                functools.partial(back_kernel, coded, (early, late), snaps),
                out_shape=(map_shape, energy_shape),
                in_specs=[smem()] * 4 + [vmem()] * (4 + len(received)),
                out_specs=(vmem(),) * 2,
                scratch_shapes=[pltpu.VMEM(slot_shape.shape, F32)],
                compiler_params=grant,
            )(info, step_size, entries, more, contrib, current, chosen, held, *received)
        energies = [energy] + [
            lax.ppermute(energy, "bin", [(i, (i + k) % groups) for i in range(groups)])
            for k in range(1, groups)
        ]
        if iteration < ITERS - 1:
            current, contrib, sent = pl.pallas_call(
                functools.partial(next_kernel, groups, snaps),
                out_shape=(map_shape, slot_shape, sent_shape),
                in_specs=[smem()] * 2 + [vmem()] * (3 + groups),
                out_specs=(vmem(),) * 3,
                scratch_shapes=[masked],
                compiler_params=grant,
            )(info, step_size, moved, *energies, pen, held)
    return pl.pallas_call(
        functools.partial(last_kernel, groups, snaps),
        out_shape=shape(initial_map.shape, F32),
        in_specs=[smem()] + [vmem()] * (2 + groups),
        out_specs=vmem(),
        compiler_params=grant,
    )(step_size, moved, *energies, pen)


def solution(mesh):
    in_specs = (
        P("scan", "bin", None, None),
        P(None, "scan"),
        P("scan"),
        P("bin", None, "scan"),
        P("bin", None, "scan"),
        P(),
        P("scan"),
    )
    run = functools.partial(body, mesh.shape["scan"], mesh.shape["bin"])
    return jax.shard_map(run, mesh=mesh, in_specs=in_specs, out_specs=P("bin", None, "scan"), check_vma=False)
```

```python
import functools

import jax
import jax.numpy as jnp
from jax import lax
from jax.experimental import pallas as pl
from jax.experimental.pallas import tpu as pltpu
from jax.sharding import PartitionSpec as P


ITERS = 2
BITS = 14
ROWS_AT = 128
PRODUCT_AT = 64
F32 = jnp.float32
BF16 = jnp.bfloat16
I32 = jnp.int32
I16 = jnp.int16


def partners(count, k):
    if count & (count - 1):
        return [(i, (i + k) % count) for i in range(count)]
    return [(i, i ^ k) for i in range(count)]


def vmem():
    return pl.BlockSpec(memory_space=pltpu.VMEM)


def smem():
    return pl.BlockSpec(memory_space=pltpu.SMEM)


def hbm():
    return pl.BlockSpec(memory_space=pltpu.HBM)


def in_hbm(value):
    return pltpu.with_memory_space_constraint(value, pltpu.HBM)


def taker(refs):
    refs = list(refs)

    def take(n):
        taken, refs[:] = refs[:n], refs[n:]
        return taken

    return take


class Info:
    def __init__(self, ref, slots):
        self.ref, self.slots = ref, slots

    @staticmethod
    def size(slots):
        return 3 * slots + 2

    def row(self, s):
        return self.ref[s]

    def col(self, s):
        return self.ref[self.slots + s]

    def first(self, s):
        return self.ref[2 * self.slots + s]

    def shared(self):
        return self.ref[3 * self.slots]

    def live(self):
        return self.ref[3 * self.slots + 1]

    def fill(self, pattern_ref, count_ref, columns):
        slots, live = self.slots, count_ref[0]
        rows = [pattern_ref[0, s] for s in range(slots)]
        flag = jnp.int32(0)
        for s in range(slots):
            first = jnp.int32(s)
            for t in range(s - 1, -1, -1):
                first = jnp.where((rows[t] == rows[s]) & (s < live), t, first)
            self.ref[s] = rows[s]
            self.ref[slots + s] = lax.rem(pattern_ref[1, s], columns)
            self.ref[2 * slots + s] = first
            flag = flag | (first < s).astype(I32)
        self.ref[3 * slots] = flag
        self.ref[3 * slots + 1] = live


def start_tiles(a_hbm, a_ref, sems, low, high):
    copies = [pltpu.make_async_copy(a_hbm.at[s], a_ref.at[s], sems.at[s]) for s in range(low, high)]
    for copy in copies:
        copy.start()
    return copies


def masked_rows(value, bins, snaps):
    row = lax.broadcasted_iota(I32, value.shape, 0) // snaps
    return [jnp.where(row == f, value, 0.0).astype(BF16) for f in range(bins)]


def encode(value):
    top = jnp.max(jnp.abs(value), axis=1, keepdims=True)
    power = jnp.clip(jnp.ceil(jnp.log2(jnp.maximum(top, 1e-30))), -100.0, 127.0)
    code = jnp.clip(jnp.round(value * jnp.exp2(BITS - power)), -32767.0, 32767.0)
    return code.astype(I32).astype(I16), power.astype(I32)


def decode(code, note, lane, at):
    power = jnp.sum(jnp.where(lane == at, note, 0.0), axis=1, keepdims=True)
    return code.astype(I32).astype(F32) * jnp.exp2(power - BITS)


def forward(value, snaps, info, waits, xm_ref, a_ref, c_ref):
    slots, bins, tile = a_ref.shape[0], a_ref.shape[1], a_ref.shape[-1]
    for f, part in enumerate(masked_rows(value, bins, snaps)):
        xm_ref[f] = part
    for s in range(slots):
        for copy in waits.get(s, ()):
            copy.wait()
        start = pl.multiple_of(info.col(s) * tile, tile)
        total = None
        for f in range(bins):
            part = lax.dot_general(
                xm_ref[f, :, pl.ds(start, tile)],
                a_ref[s, f],
                (((1,), (1,)), ((), ())),
                preferred_element_type=F32,
            )
            total = part if total is None else total + part
        c_ref[s] = total

    @pl.when(info.shared() > 0)
    def _():
        for s in range(1, slots):
            first = info.first(s)

            @pl.when(first < s)
            def _():
                c_ref[first] += c_ref[s]


def start_kernel(coded, columns, count_ref, pattern_hbm, x_hbm, m_hbm, a_hbm, *refs):
    cur_ref, c_ref, out_ref, info_ref, pattern_ref, x_ref, m_ref, a_ref, xm_ref, small, sems = refs
    slots = a_ref.shape[0]
    bins, snaps = x_ref.shape[:2]
    loads = [
        pltpu.make_async_copy(source, target, small.at[i])
        for i, (source, target) in enumerate(
            [(pattern_hbm, pattern_ref), (x_hbm, x_ref), (m_hbm, m_ref)]
        )
    ]
    for load in loads:
        load.start()
    copies = start_tiles(a_hbm, a_ref, sems, 0, slots * 3 // 4)
    loads[0].wait()
    info = Info(info_ref, slots)
    info.fill(pattern_ref, count_ref, columns)
    loads[1].wait()
    value = jnp.concatenate([x_ref[f] for f in range(bins)], axis=0)
    cur_ref[...] = value
    copies += start_tiles(a_hbm, a_ref, sems, slots * 3 // 4, slots)
    waits = {0: copies[: slots * 3 // 4], slots * 3 // 4: copies[slots * 3 // 4 :]}
    loads[2].wait()
    lanes, tile = out_ref.shape[1:]
    if coded:
        own = out_ref.shape[0] - slots - 1
        lane = lax.broadcasted_iota(I32, (lanes, tile), 1)
        note = jnp.full((lanes, tile), -1, I32)
        for b in range(own):
            code, power = encode(
                jnp.concatenate([m_ref[f, :, b * tile : (b + 1) * tile] for f in range(bins)], axis=0)
            )
            out_ref[b] = code
            note = jnp.where(lane == b, power, note)
        for s in range(slots):
            keep = (s < info.live()) & (info.first(s) == s)
            note = jnp.where((lane == ROWS_AT + s) & keep, info.row(s), note)
    forward(value, snaps, info, waits, xm_ref, a_ref, c_ref)
    for s in range(slots):
        if coded:
            code, power = encode(c_ref[s])
            out_ref[own + s] = code
            note = jnp.where(lane == PRODUCT_AT + s, power, note)
        else:
            out_ref[s] = c_ref[s].astype(BF16)
    if coded:
        out_ref[own + slots] = note.astype(I16)


def shrink(moved, energies, step, penalty):
    energy = energies[0]
    for other in energies[1:]:
        energy = energy + other
    return moved * jnp.maximum(0.0, 1.0 - step * penalty / jnp.sqrt(energy + 1e-6))


def next_kernel(groups, snaps, *refs):
    take = taker(refs)
    info_ref, step_ref, moved_ref = take(3)
    energy_refs = take(groups)
    penalty_ref, a_ref, cur_ref, c_ref, out_ref, xm_ref = take(6)
    slots = a_ref.shape[0]
    value = shrink(moved_ref[...], [e[...] for e in energy_refs], step_ref[0], penalty_ref[...])
    cur_ref[...] = value
    forward(value, snaps, Info(info_ref, slots), {}, xm_ref, a_ref, c_ref)
    for s in range(slots):
        out_ref[s] = c_ref[s].astype(BF16)


def last_kernel(groups, snaps, *refs):
    take = taker(refs)
    step_ref, moved_ref = take(2)
    energy_refs = take(groups)
    penalty_ref, out_ref = take(2)
    value = shrink(moved_ref[...], [e[...] for e in energy_refs], step_ref[0], penalty_ref[...])
    for f in range(out_ref.shape[0]):
        out_ref[f] = value[f * snaps : (f + 1) * snaps]


def find_common(info, steps, slots, me, rows, order_ref, table, sem, entries_ref):
    sources = rows.shape[0]
    other = lax.broadcasted_iota(I32, rows.shape, 0)
    if steps is not None:
        far = jnp.zeros(rows.shape, I32)
        for i, k in enumerate(steps):
            far = jnp.where(other == i, k, far)
        other = far ^ me
    found = jnp.full(rows.shape, -1, I32)
    for s in range(slots):
        row = jnp.where((s < info.live()) & (info.first(s) == s), info.row(s), -2)
        found = jnp.where(rows == row, s, found)
    order_ref[...] = jnp.where(other == me, -1, found)
    copy = pltpu.make_async_copy(order_ref, table, sem)
    copy.start()

    def finish():
        copy.wait()

        def one(k, number):
            entries_ref[k] = number
            for t in range(slots):
                slot = table[k, t]
                entries_ref[number] = (t if steps is not None else k * slots + t) * 64 + slot
                number = number + (slot >= 0).astype(I32)
            return number

        entries_ref[sources] = lax.fori_loop(0, sources, one, jnp.int32(sources + 1))

    return finish


def gradient(info, columns, snaps, a_ref, r_ref):
    slots, bins, tile = a_ref.shape[0], a_ref.shape[1], a_ref.shape[-1]
    sums = [jnp.zeros((bins * snaps, tile), F32) for _ in range(columns)]
    for s in range(slots):
        value = jnp.where(s < info.live(), r_ref[info.first(s)], 0.0)
        lhs = jnp.concatenate(masked_rows(value, bins, snaps), axis=1)
        part = jnp.dot(lhs, a_ref[s].reshape(bins * tile, tile), preferred_element_type=F32)
        sums = [total + jnp.where(info.col(s) == i, part, 0.0) for i, total in enumerate(sums)]
    return jnp.concatenate(sums, axis=1)


def finish_step(cur_ref, step_ref, grad, moved_ref, energy_ref):
    moved = cur_ref[...] - step_ref[0] * grad
    moved_ref[...] = moved
    energy_ref[...] = jnp.sum(moved * moved, axis=0, keepdims=True)


def take_in(steps, refs, info, me, rows_ref, order_ref, table, sem, entries_ref, sel_ref, r_ref):
    slots = r_ref.shape[0]
    last = refs[0].shape[0] - 1
    own = last - slots
    for i, ref in enumerate(refs):
        rows_ref[i : i + 1] = ref[last, 0:1, ROWS_AT : ROWS_AT + 128].astype(I32)
    finish = find_common(info, steps, slots, me, rows_ref[...], order_ref, table, sem, entries_ref)
    lane = lax.broadcasted_iota(I32, refs[0].shape[1:], 1)
    homes = [lax.bitwise_xor(me, lax.div(info.row(s), own)) for s in range(slots)]
    for k, ref in zip(steps, refs):
        some = homes[0] == k
        for home in homes[1:]:
            some = some | (home == k)

        @pl.when(some)
        def _(k=k, ref=ref):
            note = ref[last].astype(I32).astype(F32)
            for s in range(slots):

                @pl.when(homes[s] == k)
                def _(s=s):
                    at = lax.rem(info.row(s), own)
                    value = decode(ref[at], note, lane, at)
                    sel_ref[s] = value
                    r_ref[s] -= value

    finish()
    for i, ref in enumerate(refs):

        def add(j, _, ref=ref):
            at, slot = lax.shift_right_logical(entries_ref[j], 6), entries_ref[j] & 63
            note = ref[last].astype(I32).astype(F32)
            r_ref[slot] += decode(ref[own + at], note, lane, PRODUCT_AT + at)
            return 0

        lax.fori_loop(entries_ref[i], entries_ref[i + 1], add, 0)


def early_kernel(coded, steps, *refs):
    take = taker(refs)
    info_ref, me_ref, c_ref, a_hbm = take(4)
    arrived = take(len(steps) if coded else 3)
    r_ref, sel_ref, a_ref, entries_ref, rows_ref, order_ref, table, sem, sems = take(9)
    slots = a_ref.shape[0]
    info = Info(info_ref, slots)
    me = me_ref[0]
    copies = start_tiles(a_hbm, a_ref, sems, 0, slots)
    r_ref[...] = c_ref[...]
    sel_ref[...] = jnp.zeros_like(sel_ref)
    if coded:
        take_in(steps, arrived, info, me, rows_ref, order_ref, table, sem, entries_ref, sel_ref, r_ref)
    else:
        full_ref, table_ref, recv_ref = arrived
        finish = find_common(info, None, slots, me, table_ref[...], order_ref, table, sem, entries_ref)
        for s in range(slots):
            sel_ref[s] = full_ref[info.row(s)]
            r_ref[s] -= sel_ref[s]
        finish()
        add_blocks(entries_ref, 0, table_ref.shape[0], recv_ref, r_ref)
    for copy in copies:
        copy.wait()


def late_kernel(steps, snaps, *refs):
    take = taker(refs)
    info_ref, step_ref, me_ref, part_ref, some_ref, cur_ref, a_ref = take(7)
    arrived = take(len(steps))
    moved_ref, energy_ref, sel_ref, entries_ref, r_ref = take(5)
    slots, tile = a_ref.shape[0], a_ref.shape[-1]
    info = Info(info_ref, slots)
    r_ref[...] = part_ref[...]
    sel_ref[...] = some_ref[...]
    if steps:
        rows_ref, order_ref, table, sem = take(4)
        take_in(steps, arrived, info, me_ref[0], rows_ref, order_ref, table, sem, entries_ref, sel_ref, r_ref)
    else:
        entries_ref[0] = 1
    grad = gradient(info, cur_ref.shape[1] // tile, snaps, a_ref, r_ref)
    finish_step(cur_ref, step_ref, grad, moved_ref, energy_ref)


def add_blocks(entries_ref, low, high, ref, r_ref):
    def add(i, _):
        at, slot = lax.shift_right_logical(entries_ref[i], 6), entries_ref[i] & 63
        r_ref[slot] += ref[at].astype(F32)
        return 0

    lax.fori_loop(entries_ref[low], entries_ref[high], add, 0)


def back_kernel(coded, steps, snaps, *refs):
    take = taker(refs)
    info_ref, step_ref = take(2)
    entry_refs = take(len(steps))
    c_ref, cur_ref, sel_ref, a_ref = take(4)
    arrived = dict(enumerate(take(max(k for part in steps for k in part) if coded else 1), 1))
    moved_ref, energy_ref, r_ref = take(3)
    slots, tile = a_ref.shape[0], a_ref.shape[-1]
    info = Info(info_ref, slots)
    for s in range(slots):
        r_ref[s] = c_ref[s] - sel_ref[s]
    if coded:
        for entries_ref, part in zip(entry_refs, steps):
            for i, k in enumerate(part):
                if k:
                    add_blocks(entries_ref, i, i + 1, arrived[k], r_ref)
    else:
        add_blocks(entry_refs[0], 0, arrived[1].shape[0] // slots, arrived[1], r_ref)
    grad = gradient(info, cur_ref.shape[1] // tile, snaps, a_ref, r_ref)
    finish_step(cur_ref, step_ref, grad, moved_ref, energy_ref)


def body(count, groups, tile_blocks, tile_pattern, tile_count, initial_map, measured, step_size, penalty):
    slots, bins, tile, _ = tile_blocks.shape
    snaps, points = initial_map.shape[1:]
    lanes = bins * snaps
    sensors_dev = measured.shape[2]
    blocks = sensors_dev * count // tile
    columns = points // tile
    own = sensors_dev // tile
    me = lax.axis_index("scan").astype(I32)[None]
    shape = jax.ShapeDtypeStruct
    grant = pltpu.CompilerParams(vmem_limit_bytes=20 << 20)
    coded = (
        count <= 8
        and count & (count - 1) == 0
        and sensors_dev % tile == 0
        and own <= PRODUCT_AT
        and slots < 64
        and tile >= ROWS_AT + 128
    )
    map_shape = shape((lanes, points), F32)
    slot_shape = shape((slots, lanes, tile), F32)
    sent_shape = shape((slots, lanes, tile), BF16)
    tile_shape = shape(tile_blocks.shape, BF16)
    masked = pltpu.VMEM((bins, lanes, points), BF16)
    tile_sems = pltpu.SemaphoreType.DMA((slots,))

    def swap(value, k):
        return lax.ppermute(value, "scan", [(i, i ^ k) for i in range(count)])

    def spread(value):
        if not coded:
            return [lax.all_gather(value, "scan", axis=0, tiled=True)]
        got = {}
        for k in range(2, count, 2):
            got[k] = swap(value, k)
        got[1] = swap(value, 1)
        for k in range(2, count, 2):
            got[k + 1] = swap(got[k], 1)
        return [got[k] for k in range(1, count)]

    current, contrib, sent, info = pl.pallas_call(
        functools.partial(start_kernel, coded, columns),
        out_shape=(
            map_shape,
            slot_shape,
            shape((own + slots + 1, lanes, tile), I16) if coded else sent_shape,
            shape((Info.size(slots),), I32),
        ),
        in_specs=[smem()] + [hbm()] * 4,
        out_specs=(vmem(), vmem(), vmem(), smem()),
        scratch_shapes=[
            pltpu.SMEM(tile_pattern.shape, I32),
            pltpu.VMEM(initial_map.shape, F32),
            pltpu.VMEM(measured.shape, F32),
            pltpu.VMEM(tile_blocks.shape, BF16),
            masked,
            pltpu.SemaphoreType.DMA((3,)),
            tile_sems,
        ],
        compiler_params=grant,
    )(tile_count, in_hbm(tile_pattern), in_hbm(initial_map), in_hbm(measured), in_hbm(tile_blocks))

    late = list(range(5, count, 2)) if coded else []
    early = [k for k in range(count) if k not in late] if coded else []
    if coded:
        given = [sent] + spread(sent)
        ready, waiting = [given[k] for k in early], [given[k] for k in late]
    else:
        full = lax.all_gather(measured, "scan", axis=2, tiled=True)
        order = jnp.arange(slots, dtype=I32)
        keep = (order < tile_count[0]) & (info[2 * slots : 3 * slots] == order)
        rows = jnp.pad(jnp.where(keep, tile_pattern[0], -1), (0, 128 - slots), constant_values=-1)
        ready = [
            full.reshape(lanes, blocks, tile).transpose(1, 0, 2),
            lax.all_gather(rows[None], "scan", axis=0, tiled=True),
        ] + spread(sent)
        waiting = []

    def plan_scratch(sources):
        return [
            pltpu.VMEM((sources, 128), I32),
            pltpu.VMEM((sources, 128), I32),
            pltpu.SMEM((sources, 128), I32),
            pltpu.SemaphoreType.DMA,
        ]

    def entries_shape(sources):
        return shape((sources + 2 + sources * slots,), I32)

    pen = penalty.reshape(1, points)
    energy_shape = shape((1, points), F32)
    for iteration in range(ITERS):
        if iteration == 0:
            sources = len(early) if coded else count
            partial, some, held, entries = pl.pallas_call(
                functools.partial(early_kernel, coded, early),
                out_shape=(slot_shape, slot_shape, tile_shape, entries_shape(sources)),
                in_specs=[smem()] * 2 + [vmem(), hbm()] + [vmem()] * len(ready),
                out_specs=(vmem(),) * 3 + (smem(),),
                scratch_shapes=plan_scratch(sources) + [tile_sems],
                compiler_params=grant,
            )(info, me, contrib, in_hbm(tile_blocks), *ready)
            moved, energy, chosen, more = pl.pallas_call(
                functools.partial(late_kernel, late, snaps),
                out_shape=(map_shape, energy_shape, slot_shape, entries_shape(len(late))),
                in_specs=[smem()] * 3 + [vmem()] * (4 + len(waiting)),
                out_specs=(vmem(),) * 3 + (smem(),),
                scratch_shapes=[pltpu.VMEM(slot_shape.shape, F32)] + (plan_scratch(len(late)) if late else []),
                compiler_params=grant,
            )(info, step_size, me, partial, some, current, held, *waiting)
        else:
            received = spread(sent)
            moved, energy = pl.pallas_call(
                functools.partial(back_kernel, coded, (early, late), snaps),
                out_shape=(map_shape, energy_shape),
                in_specs=[smem()] * 4 + [vmem()] * (4 + len(received)),
                out_specs=(vmem(),) * 2,
                scratch_shapes=[pltpu.VMEM(slot_shape.shape, F32)],
                compiler_params=grant,
            )(info, step_size, entries, more, contrib, current, chosen, held, *received)
        energies = [energy] + [
            lax.ppermute(energy, "bin", partners(groups, k))
            for k in range(1, groups)
        ]
        if iteration < ITERS - 1:
            current, contrib, sent = pl.pallas_call(
                functools.partial(next_kernel, groups, snaps),
                out_shape=(map_shape, slot_shape, sent_shape),
                in_specs=[smem()] * 2 + [vmem()] * (3 + groups),
                out_specs=(vmem(),) * 3,
                scratch_shapes=[masked],
                compiler_params=grant,
            )(info, step_size, moved, *energies, pen, held)
    return pl.pallas_call(
        functools.partial(last_kernel, groups, snaps),
        out_shape=shape(initial_map.shape, F32),
        in_specs=[smem()] + [vmem()] * (2 + groups),
        out_specs=vmem(),
        compiler_params=grant,
    )(step_size, moved, *energies, pen)


def solution(mesh):
    in_specs = (
        P("scan", "bin", None, None),
        P(None, "scan"),
        P("scan"),
        P("bin", None, "scan"),
        P("bin", None, "scan"),
        P(),
        P("scan"),
    )
    count = mesh.shape["scan"]

    def run(*args):
        return body(count, mesh.shape["bin"], *args)

    return jax.shard_map(run, mesh=mesh, in_specs=in_specs, out_specs=P("bin", None, "scan"), check_vma=False)
```

```python
import functools

import jax
import jax.numpy as jnp
from jax import lax
from jax.experimental import pallas as pl
from jax.experimental.pallas import tpu as pltpu
from jax.sharding import PartitionSpec as P


ITERS = 2
BITS = 14
ROWS_AT = 128
PRODUCT_AT = 64
F32 = jnp.float32
BF16 = jnp.bfloat16
I32 = jnp.int32
I16 = jnp.int16


def partners(count, k):
    if count & (count - 1):
        return [(i, (i + k) % count) for i in range(count)]
    return [(i, i ^ k) for i in range(count)]


def vmem():
    return pl.BlockSpec(memory_space=pltpu.VMEM)


def smem():
    return pl.BlockSpec(memory_space=pltpu.SMEM)


def hbm():
    return pl.BlockSpec(memory_space=pltpu.HBM)


def in_hbm(value):
    return pltpu.with_memory_space_constraint(value, pltpu.HBM)


def taker(refs):
    refs = list(refs)

    def take(n):
        taken, refs[:] = refs[:n], refs[n:]
        return taken

    return take


class Info:
    def __init__(self, ref, slots):
        self.ref, self.slots = ref, slots

    @staticmethod
    def size(slots):
        return 3 * slots + 2

    def row(self, s):
        return self.ref[s]

    def col(self, s):
        return self.ref[self.slots + s]

    def first(self, s):
        return self.ref[2 * self.slots + s]

    def shared(self):
        return self.ref[3 * self.slots]

    def live(self):
        return self.ref[3 * self.slots + 1]

    def fill(self, pattern_ref, count_ref, columns):
        slots, live = self.slots, count_ref[0]
        rows = [pattern_ref[0, s] for s in range(slots)]
        flag = jnp.int32(0)
        for s in range(slots):
            first = jnp.int32(s)
            for t in range(s - 1, -1, -1):
                first = jnp.where((rows[t] == rows[s]) & (s < live), t, first)
            self.ref[s] = rows[s]
            self.ref[slots + s] = lax.rem(pattern_ref[1, s], columns)
            self.ref[2 * slots + s] = first
            flag = flag | (first < s).astype(I32)
        self.ref[3 * slots] = flag
        self.ref[3 * slots + 1] = live


def start_tiles(a_hbm, a_ref, sems, low, high):
    copies = [pltpu.make_async_copy(a_hbm.at[s], a_ref.at[s], sems.at[s]) for s in range(low, high)]
    for copy in copies:
        copy.start()
    return copies


def masked_rows(value, bins, snaps):
    row = lax.broadcasted_iota(I32, value.shape, 0) // snaps
    return [jnp.where(row == f, value, 0.0).astype(BF16) for f in range(bins)]


def encode(value):
    top = jnp.max(jnp.abs(value), axis=1, keepdims=True)
    power = jnp.clip(jnp.ceil(jnp.log2(jnp.maximum(top, 1e-30))), -100.0, 127.0)
    code = jnp.clip(jnp.round(value * jnp.exp2(BITS - power)), -32767.0, 32767.0)
    return code.astype(I32).astype(I16), power.astype(I32)


def decode(code, note, lane, at):
    power = jnp.sum(jnp.where(lane == at, note, 0.0), axis=1, keepdims=True)
    return code.astype(I32).astype(F32) * jnp.exp2(power - BITS)


def forward(value, snaps, info, waits, xm_ref, a_ref, c_ref):
    slots, bins, tile = a_ref.shape[0], a_ref.shape[1], a_ref.shape[-1]
    for f, part in enumerate(masked_rows(value, bins, snaps)):
        xm_ref[f] = part
    for s in range(slots):
        for copy in waits.get(s, ()):
            copy.wait()
        start = pl.multiple_of(info.col(s) * tile, tile)
        total = None
        for f in range(bins):
            part = lax.dot_general(
                xm_ref[f, :, pl.ds(start, tile)],
                a_ref[s, f],
                (((1,), (1,)), ((), ())),
                preferred_element_type=F32,
            )
            total = part if total is None else total + part
        c_ref[s] = total

    @pl.when(info.shared() > 0)
    def _():
        for s in range(1, slots):
            first = info.first(s)

            @pl.when(first < s)
            def _():
                c_ref[first] += c_ref[s]


def start_kernel(coded, columns, count_ref, pattern_hbm, x_hbm, m_hbm, a_hbm, *refs):
    cur_ref, c_ref, out_ref, info_ref, pattern_ref, x_ref, m_ref, a_ref, xm_ref, small, sems = refs
    slots = a_ref.shape[0]
    bins, snaps = x_ref.shape[:2]
    loads = [
        pltpu.make_async_copy(source, target, small.at[i])
        for i, (source, target) in enumerate(
            [(pattern_hbm, pattern_ref), (x_hbm, x_ref), (m_hbm, m_ref)]
        )
    ]
    for load in loads:
        load.start()
    copies = start_tiles(a_hbm, a_ref, sems, 0, slots * 3 // 4)
    loads[0].wait()
    info = Info(info_ref, slots)
    info.fill(pattern_ref, count_ref, columns)
    loads[1].wait()
    value = jnp.concatenate([x_ref[f] for f in range(bins)], axis=0)
    cur_ref[...] = value
    copies += start_tiles(a_hbm, a_ref, sems, slots * 3 // 4, slots)
    waits = {0: copies[: slots * 3 // 4], slots * 3 // 4: copies[slots * 3 // 4 :]}
    loads[2].wait()
    lanes, tile = out_ref.shape[1:]
    if coded:
        own = out_ref.shape[0] - slots - 1
        lane = lax.broadcasted_iota(I32, (lanes, tile), 1)
        note = jnp.full((lanes, tile), -1, I32)
        for b in range(own):
            code, power = encode(
                jnp.concatenate([m_ref[f, :, b * tile : (b + 1) * tile] for f in range(bins)], axis=0)
            )
            out_ref[b] = code
            note = jnp.where(lane == b, power, note)
        for s in range(slots):
            keep = (s < info.live()) & (info.first(s) == s)
            note = jnp.where((lane == ROWS_AT + s) & keep, info.row(s), note)
    forward(value, snaps, info, waits, xm_ref, a_ref, c_ref)
    for s in range(slots):
        if coded:
            code, power = encode(c_ref[s])
            out_ref[own + s] = code
            note = jnp.where(lane == PRODUCT_AT + s, power, note)
        else:
            out_ref[s] = c_ref[s].astype(BF16)
    if coded:
        out_ref[own + slots] = note.astype(I16)


def shrink(moved, energies, step, penalty):
    energy = energies[0]
    for other in energies[1:]:
        energy = energy + other
    return moved * jnp.maximum(0.0, 1.0 - step * penalty / jnp.sqrt(energy + 1e-6))


def next_kernel(groups, snaps, *refs):
    take = taker(refs)
    info_ref, step_ref, moved_ref = take(3)
    energy_refs = take(groups)
    penalty_ref, a_ref, cur_ref, c_ref, out_ref, xm_ref = take(6)
    slots = a_ref.shape[0]
    value = shrink(moved_ref[...], [e[...] for e in energy_refs], step_ref[0], penalty_ref[...])
    cur_ref[...] = value
    forward(value, snaps, Info(info_ref, slots), {}, xm_ref, a_ref, c_ref)
    for s in range(slots):
        out_ref[s] = c_ref[s].astype(BF16)


def last_kernel(groups, snaps, *refs):
    take = taker(refs)
    step_ref, moved_ref = take(2)
    energy_refs = take(groups)
    penalty_ref, out_ref = take(2)
    value = shrink(moved_ref[...], [e[...] for e in energy_refs], step_ref[0], penalty_ref[...])
    for f in range(out_ref.shape[0]):
        out_ref[f] = value[f * snaps : (f + 1) * snaps]


def find_common(info, steps, slots, me, rows, order_ref, table, sem, entries_ref):
    sources = rows.shape[0]
    other = lax.broadcasted_iota(I32, rows.shape, 0)
    if steps is not None:
        far = jnp.zeros(rows.shape, I32)
        for i, k in enumerate(steps):
            far = jnp.where(other == i, k, far)
        other = far ^ me
    found = jnp.full(rows.shape, -1, I32)
    for s in range(slots):
        row = jnp.where((s < info.live()) & (info.first(s) == s), info.row(s), -2)
        found = jnp.where(rows == row, s, found)
    order_ref[...] = jnp.where(other == me, -1, found)
    copy = pltpu.make_async_copy(order_ref, table, sem)
    copy.start()

    def finish():
        copy.wait()

        def one(k, number):
            entries_ref[k] = number
            for t in range(slots):
                slot = table[k, t]
                entries_ref[number] = (t if steps is not None else k * slots + t) * 64 + slot
                number = number + (slot >= 0).astype(I32)
            return number

        entries_ref[sources] = lax.fori_loop(0, sources, one, jnp.int32(sources + 1))

    return finish


def gradient(info, columns, snaps, a_ref, r_ref):
    slots, bins, tile = a_ref.shape[0], a_ref.shape[1], a_ref.shape[-1]
    sums = [jnp.zeros((bins * snaps, tile), F32) for _ in range(columns)]
    for s in range(slots):
        value = jnp.where(s < info.live(), r_ref[info.first(s)], 0.0)
        lhs = jnp.concatenate(masked_rows(value, bins, snaps), axis=1)
        part = jnp.dot(lhs, a_ref[s].reshape(bins * tile, tile), preferred_element_type=F32)
        sums = [total + jnp.where(info.col(s) == i, part, 0.0) for i, total in enumerate(sums)]
    return jnp.concatenate(sums, axis=1)


def finish_step(cur_ref, step_ref, grad, moved_ref, energy_ref):
    moved = cur_ref[...] - step_ref[0] * grad
    moved_ref[...] = moved
    energy_ref[...] = jnp.sum(moved * moved, axis=0, keepdims=True)


def take_in(steps, refs, info, me, rows_ref, order_ref, table, sem, entries_ref, sel_ref, r_ref):
    slots = r_ref.shape[0]
    last = refs[0].shape[0] - 1
    own = last - slots
    for i, ref in enumerate(refs):
        rows_ref[i : i + 1] = ref[last, 0:1, ROWS_AT : ROWS_AT + 128].astype(I32)
    finish = find_common(info, steps, slots, me, rows_ref[...], order_ref, table, sem, entries_ref)
    lane = lax.broadcasted_iota(I32, refs[0].shape[1:], 1)
    homes = [lax.bitwise_xor(me, lax.div(info.row(s), own)) for s in range(slots)]
    for k, ref in zip(steps, refs):
        some = homes[0] == k
        for home in homes[1:]:
            some = some | (home == k)

        @pl.when(some)
        def _(k=k, ref=ref):
            note = ref[last].astype(I32).astype(F32)
            for s in range(slots):

                @pl.when(homes[s] == k)
                def _(s=s):
                    at = lax.rem(info.row(s), own)
                    value = decode(ref[at], note, lane, at)
                    sel_ref[s] = value
                    r_ref[s] -= value

    finish()
    for i, ref in enumerate(refs):

        def add(j, _, ref=ref):
            at, slot = lax.shift_right_logical(entries_ref[j], 6), entries_ref[j] & 63
            note = ref[last].astype(I32).astype(F32)
            r_ref[slot] += decode(ref[own + at], note, lane, PRODUCT_AT + at)
            return 0

        lax.fori_loop(entries_ref[i], entries_ref[i + 1], add, 0)


def early_kernel(coded, steps, *refs):
    take = taker(refs)
    info_ref, me_ref, c_ref, a_hbm = take(4)
    arrived = take(len(steps) if coded else 3)
    r_ref, sel_ref, a_ref, entries_ref, rows_ref, order_ref, table, sem, sems = take(9)
    slots = a_ref.shape[0]
    info = Info(info_ref, slots)
    me = me_ref[0]
    copies = start_tiles(a_hbm, a_ref, sems, 0, slots)
    r_ref[...] = c_ref[...]
    sel_ref[...] = jnp.zeros_like(sel_ref)
    if coded:
        take_in(steps, arrived, info, me, rows_ref, order_ref, table, sem, entries_ref, sel_ref, r_ref)
    else:
        full_ref, table_ref, recv_ref = arrived
        finish = find_common(info, None, slots, me, table_ref[...], order_ref, table, sem, entries_ref)
        for s in range(slots):
            sel_ref[s] = full_ref[info.row(s)]
            r_ref[s] -= sel_ref[s]
        finish()
        add_blocks(entries_ref, 0, table_ref.shape[0], recv_ref, r_ref)
    for copy in copies:
        copy.wait()


def late_kernel(steps, snaps, *refs):
    take = taker(refs)
    info_ref, step_ref, me_ref, part_ref, some_ref, cur_ref, a_ref = take(7)
    arrived = take(len(steps))
    moved_ref, energy_ref, sel_ref, entries_ref, r_ref = take(5)
    slots, tile = a_ref.shape[0], a_ref.shape[-1]
    info = Info(info_ref, slots)
    r_ref[...] = part_ref[...]
    sel_ref[...] = some_ref[...]
    if steps:
        rows_ref, order_ref, table, sem = take(4)
        take_in(steps, arrived, info, me_ref[0], rows_ref, order_ref, table, sem, entries_ref, sel_ref, r_ref)
    else:
        entries_ref[0] = 1
    grad = gradient(info, cur_ref.shape[1] // tile, snaps, a_ref, r_ref)
    finish_step(cur_ref, step_ref, grad, moved_ref, energy_ref)


def add_blocks(entries_ref, low, high, ref, r_ref):
    def add(i, _):
        at, slot = lax.shift_right_logical(entries_ref[i], 6), entries_ref[i] & 63
        r_ref[slot] += ref[at].astype(F32)
        return 0

    lax.fori_loop(entries_ref[low], entries_ref[high], add, 0)


def back_kernel(coded, steps, snaps, *refs):
    take = taker(refs)
    info_ref, step_ref = take(2)
    entry_refs = take(len(steps))
    c_ref, cur_ref, sel_ref, a_ref = take(4)
    arrived = dict(enumerate(take(max(k for part in steps for k in part) if coded else 1), 1))
    moved_ref, energy_ref, r_ref = take(3)
    slots, tile = a_ref.shape[0], a_ref.shape[-1]
    info = Info(info_ref, slots)
    for s in range(slots):
        r_ref[s] = c_ref[s] - sel_ref[s]
    if coded:
        for entries_ref, part in zip(entry_refs, steps):
            for i, k in enumerate(part):
                if k:
                    add_blocks(entries_ref, i, i + 1, arrived[k], r_ref)
    else:
        add_blocks(entry_refs[0], 0, arrived[1].shape[0] // slots, arrived[1], r_ref)
    grad = gradient(info, cur_ref.shape[1] // tile, snaps, a_ref, r_ref)
    finish_step(cur_ref, step_ref, grad, moved_ref, energy_ref)


def body(count, groups, tile_blocks, tile_pattern, tile_count, initial_map, measured, step_size, penalty):
    slots, bins, tile, _ = tile_blocks.shape
    snaps, points = initial_map.shape[1:]
    lanes = bins * snaps
    sensors_dev = measured.shape[2]
    blocks = sensors_dev * count // tile
    columns = points // tile
    own = sensors_dev // tile
    me = lax.axis_index("scan").astype(I32)[None]
    shape = jax.ShapeDtypeStruct
    grant = pltpu.CompilerParams(vmem_limit_bytes=20 << 20)
    coded = (
        count <= 8
        and count & (count - 1) == 0
        and sensors_dev % tile == 0
        and own <= PRODUCT_AT
        and slots < 64
        and tile >= ROWS_AT + 128
    )
    map_shape = shape((lanes, points), F32)
    slot_shape = shape((slots, lanes, tile), F32)
    sent_shape = shape((slots, lanes, tile), BF16)
    tile_shape = shape(tile_blocks.shape, BF16)
    masked = pltpu.VMEM((bins, lanes, points), BF16)
    tile_sems = pltpu.SemaphoreType.DMA((slots,))

    def swap(value, k):
        return lax.ppermute(value, "scan", [(i, i ^ k) for i in range(count)])

    def spread(value):
        if not coded:
            return [lax.all_gather(value, "scan", axis=0, tiled=True)]
        got = {}
        for k in range(2, count, 2):
            got[k] = swap(value, k)
        got[1] = swap(value, 1)
        for k in range(2, count, 2):
            got[k + 1] = swap(got[k], 1)
        return [got[k] for k in range(1, count)]

    current, contrib, sent, info = pl.pallas_call(
        functools.partial(start_kernel, coded, columns),
        out_shape=(
            map_shape,
            slot_shape,
            shape((own + slots + 1, lanes, tile), I16) if coded else sent_shape,
            shape((Info.size(slots),), I32),
        ),
        in_specs=[smem()] + [hbm()] * 4,
        out_specs=(vmem(), vmem(), vmem(), smem()),
        scratch_shapes=[
            pltpu.SMEM(tile_pattern.shape, I32),
            pltpu.VMEM(initial_map.shape, F32),
            pltpu.VMEM(measured.shape, F32),
            pltpu.VMEM(tile_blocks.shape, BF16),
            masked,
            pltpu.SemaphoreType.DMA((3,)),
            tile_sems,
        ],
        compiler_params=grant,
    )(tile_count, in_hbm(tile_pattern), in_hbm(initial_map), in_hbm(measured), in_hbm(tile_blocks))

    late = list(range(5, count, 2)) if coded else []
    early = [k for k in range(count) if k not in late] if coded else []
    if coded:
        given = [sent] + spread(sent)
        ready, waiting = [given[k] for k in early], [given[k] for k in late]
    else:
        full = lax.all_gather(measured, "scan", axis=2, tiled=True)
        order = jnp.arange(slots, dtype=I32)
        keep = (order < tile_count[0]) & (info[2 * slots : 3 * slots] == order)
        rows = jnp.pad(jnp.where(keep, tile_pattern[0], -1), (0, 128 - slots), constant_values=-1)
        ready = [
            full.reshape(lanes, blocks, tile).transpose(1, 0, 2),
            lax.all_gather(rows[None], "scan", axis=0, tiled=True),
        ] + spread(sent)
        waiting = []

    def plan_scratch(sources):
        return [
            pltpu.VMEM((sources, 128), I32),
            pltpu.VMEM((sources, 128), I32),
            pltpu.SMEM((sources, 128), I32),
            pltpu.SemaphoreType.DMA,
        ]

    def entries_shape(sources):
        return shape((sources + 2 + sources * slots,), I32)

    pen = penalty.reshape(1, points)
    energy_shape = shape((1, points), F32)
    for iteration in range(ITERS):
        if iteration == 0:
            sources = len(early) if coded else count
            partial, some, held, entries = pl.pallas_call(
                functools.partial(early_kernel, coded, early),
                out_shape=(slot_shape, slot_shape, tile_shape, entries_shape(sources)),
                in_specs=[smem()] * 2 + [vmem(), hbm()] + [vmem()] * len(ready),
                out_specs=(vmem(),) * 3 + (smem(),),
                scratch_shapes=plan_scratch(sources) + [tile_sems],
                compiler_params=grant,
            )(info, me, contrib, in_hbm(tile_blocks), *ready)
            moved, energy, chosen, more = pl.pallas_call(
                functools.partial(late_kernel, late, snaps),
                out_shape=(map_shape, energy_shape, slot_shape, entries_shape(len(late))),
                in_specs=[smem()] * 3 + [vmem()] * (4 + len(waiting)),
                out_specs=(vmem(),) * 3 + (smem(),),
                scratch_shapes=[pltpu.VMEM(slot_shape.shape, F32)] + (plan_scratch(len(late)) if late else []),
                compiler_params=grant,
            )(info, step_size, me, partial, some, current, held, *waiting)
        else:
            received = spread(sent)
            moved, energy = pl.pallas_call(
                functools.partial(back_kernel, coded, (early, late), snaps),
                out_shape=(map_shape, energy_shape),
                in_specs=[smem()] * 4 + [vmem()] * (4 + len(received)),
                out_specs=(vmem(),) * 2,
                scratch_shapes=[pltpu.VMEM(slot_shape.shape, F32)],
                compiler_params=grant,
            )(info, step_size, entries, more, contrib, current, chosen, held, *received)
        energies = [energy]
        for k in range(1, groups):
            energies.append(lax.ppermute(energy, "bin", partners(groups, k)))
        if iteration < ITERS - 1:
            current, contrib, sent = pl.pallas_call(
                functools.partial(next_kernel, groups, snaps),
                out_shape=(map_shape, slot_shape, sent_shape),
                in_specs=[smem()] * 2 + [vmem()] * (3 + groups),
                out_specs=(vmem(),) * 3,
                scratch_shapes=[masked],
                compiler_params=grant,
            )(info, step_size, moved, *energies, pen, held)
    return pl.pallas_call(
        functools.partial(last_kernel, groups, snaps),
        out_shape=shape(initial_map.shape, F32),
        in_specs=[smem()] + [vmem()] * (2 + groups),
        out_specs=vmem(),
        compiler_params=grant,
    )(step_size, moved, *energies, pen)


def solution(mesh):
    in_specs = (
        P("scan", "bin", None, None),
        P(None, "scan"),
        P("scan"),
        P("bin", None, "scan"),
        P("bin", None, "scan"),
        P(),
        P("scan"),
    )
    count = mesh.shape["scan"]

    def run(*args):
        return body(count, mesh.shape["bin"], *args)

    return jax.shard_map(run, mesh=mesh, in_specs=in_specs, out_specs=P("bin", None, "scan"), check_vma=False)
```
